32 devices in a mesh: pr: 4 (over z), pc: 8 (over y, x, core).
Axes of the slice: x: 2, y: 2, z: 4, core: 2. Of those that a mesh axis runs over, the one named last changes fastest.
Arguments:
- iterate: bfloat16 [512, 1024], P('pr', 'pc'), may hold values from -6 to 6
- previous: bfloat16 [512, 1024], P('pr', 'pc'), may hold values from -6 to 6
- right_side: float32 [512, 1024], P('pr', 'pc'), may hold values from -8 to 8
- energy_gap: float32 [512, 1024], P('pr', 'pc'), may hold values from 0.5 to 8
- occ_points: bfloat16 [512, 32768], P(None, 'pr'), may hold values from -0.375 to 0.375
- virt_points: bfloat16 [1024, 32768], P(None, 'pc'), may hold values from -0.25 to 0.25
- screening: bfloat16 [32768, 32768], P('pr', 'pc'), may hold values from -0.125 to 0.125
Outputs:
- new_iterate: float32 [512, 1024], P('pr', 'pc')
The draws below stay inside these ranges and needn't reach their ends.
All inputs are finite; a program needn't handle non-finite values.
Results may differ from the reference program's by a relative error of at most 0.0045.
Values may be sent and summed in bfloat16 or wider, within the bound.
A program may use at most 256 MiB of HBM per device.

```python
import math
import jax
import jax.numpy as jnp
from jax import lax

NO = 512
NV = 1024
NP = 32768
N_PR = 4


def raised(array, rng, source, target, shards_of, factor):
    owner, partner = [(jnp.arange(array.shape[dim]) // (array.shape[dim] // shards_of)).reshape([-1 if axis == dim else 1 for axis in range(array.ndim)]) for dim in (source, target)]
    chosen = jax.random.permutation(rng, shards_of)[partner]
    strong = (owner == chosen) | (owner == (partner + shards_of // 2) % shards_of)
    return jnp.where(strong, factor * array, array)


def block_levels(own_key, shape, pieces, least, largest):
    factor_of, own = 1.0, jax.random.fold_in(own_key, 6)
    for position, blocks in pieces:
        heights = jnp.exp(jax.random.uniform(jax.random.fold_in(own, position), (blocks,), jnp.float32, least / len(pieces), largest / len(pieces)))
        factor_of = factor_of * jnp.repeat(heights, shape[position] // blocks).reshape([-1 if axis == position else 1 for axis in range(len(shape))])
    return factor_of


def centred(stream_key, extent, scale, limit, split=(), dtype=jnp.bfloat16):
    loudness = block_levels(stream_key, extent, split, -0.22, 0.18) if split else 1.0
    array = jax.random.normal(stream_key, extent, jnp.float32) * scale * loudness
    return jnp.minimum(jnp.maximum(array, -limit), limit).astype(dtype)


def bell_draw_with(key, extent, width, limit, split, heavy, kind=jnp.bfloat16):
    array = width * jax.random.normal(key, extent, jnp.float32)
    if split:
        array = array * block_levels(key, extent, split, -0.22, 0.18)
    return jnp.clip(raised(array, jax.random.fold_in(key, 3), *heavy), -limit, limit).astype(kind)


def setup_inputs(seed: int = 0) -> dict:
    streams_of = jax.random.split(jax.random.key(seed), 8)
    return {
        "iterate": centred(streams_of[0], (NO, NV), 1.0, 6.0, ((0, 4), (1, 8))),
        "previous": centred(streams_of[1], (NO, NV), 1.0, 6.0, ((0, 4), (1, 8))),
        "right_side": centred(streams_of[2], (NO, NV), 1.0, 8.0, ((0, 4), (1, 8)), jnp.float32),
        "energy_gap": jnp.clip(jnp.exp(math.log(8.0) - 2.7725887 * jax.random.uniform(streams_of[3], (NO, NV), jnp.float32) ** block_levels(streams_of[3], (NO, NV), ((0, 4), (1, 8)), -0.2, 0.2)), 0.5, 8.0),
        "occ_points": bell_draw_with(streams_of[4], (NO, NP), NO ** -0.5, 0.375, ((1, 4),), (1, 0, 4, 2.0)),
        "virt_points": bell_draw_with(streams_of[5], (NV, NP), NV ** -0.5, 0.25, ((1, 8),), (1, 0, 8, 2.0)),
        "screening": centred(streams_of[6], (NP, NP), (NP // 16) ** -0.5, 0.125, ((0, 4), (1, 8))),
    }


relax_weight = 0.8
momentum = 0.3


def reference(iterate, previous, right_side, energy_gap, occ_points, virt_points, screening):
    half_panel = jnp.dot(iterate, virt_points, preferred_element_type=jnp.float32).astype(jnp.bfloat16)
    block_rows = NP // N_PR

    def accumulate(running, offset):
        occ_block = lax.dynamic_slice_in_dim(occ_points, offset, block_rows, 1)
        screen_block = lax.dynamic_slice_in_dim(screening, offset, block_rows, 0)
        pair_field = lax.dot_general(occ_block, half_panel, (((0,), (0,)), ((), ())), preferred_element_type=jnp.float32)
        screened = (screen_block.astype(jnp.float32) * pair_field).astype(jnp.bfloat16)
        return running + jnp.dot(occ_block, screened, preferred_element_type=jnp.float32), None

    offsets = (jnp.arange(N_PR) * block_rows).astype(jnp.int32)
    summed, unused = lax.scan(accumulate, jnp.zeros((NO, NP), jnp.float32), offsets)
    back_panel = summed.astype(jnp.bfloat16)
    kernel = lax.dot_general(back_panel, virt_points, (((1,), (1,)), ((), ())), preferred_element_type=jnp.float32)
    current = iterate.astype(jnp.float32)
    residual = right_side - energy_gap * current - kernel
    return current + relax_weight * residual / energy_gap + momentum * (current - previous.astype(jnp.float32))
```

```python
import functools

import jax
import jax.numpy as jnp
from jax import lax
from jax.experimental import pallas as pl
from jax.experimental.pallas import tpu as pltpu
from jax.sharding import PartitionSpec as P

relax_weight = 0.8
momentum = 0.3
MESH = pl.DeviceIdType.MESH
CORES = 2


def place(nr, nc):
    r, c = lax.axis_index("pr"), lax.axis_index("pc")
    chips = nc // CORES
    return r, c, c // CORES, c % CORES, chips


def greet(nr, nc):
    r, c, chip, core, chips = place(nr, nc)
    barrier = pltpu.get_barrier_semaphore()
    for d in range(1, nr):
        pl.semaphore_signal(barrier, inc=1, device_id={"pr": (r + d) % nr}, device_id_type=MESH)
    for d in range(1, chips):
        peer = ((chip + d) % chips) * CORES + core
        pl.semaphore_signal(barrier, inc=1, device_id={"pc": peer}, device_id_type=MESH)
    pl.semaphore_signal(barrier, inc=1, device_id={"pc": chip * CORES + 1 - core}, device_id_type=MESH)
    pl.semaphore_wait(barrier, nr - 1 + chips)


def remote(src, dst, send, recv, **where):
    return pltpu.make_async_remote_copy(
        src_ref=src, dst_ref=dst, send_sem=send, recv_sem=recv, device_id=where, device_id_type=MESH
    )


def gather_kernel(nr, nc, flat, x_ref, out_ref, own_sem, zs, zr, cs, cr, ps, pr_):
    r, c, chip, core, chips = place(nr, nc)
    rows, cols = x_ref.shape
    partner = chip * CORES + 1 - core

    def column(j):
        if flat:
            return out_ref.at[:, pl.ds(pl.multiple_of(j * cols, cols), cols)]
        return out_ref.at[j]

    def block(i, j):
        own = pl.ds(pl.multiple_of(i * rows, rows), rows)
        if flat:
            return out_ref.at[own, pl.ds(pl.multiple_of(j * cols, cols), cols)]
        return out_ref.at[j, own]

    greet(nr, nc)
    keep = pltpu.make_async_copy(x_ref, block(r, c), own_sem)
    keep.start()
    along = [
        remote(x_ref, block(r, c), zs.at[d - 1], zr.at[d - 1], pr=(r + d) % nr) for d in range(1, nr)
    ]
    for copy in along:
        copy.start()
    keep.wait()
    for d in range(1, nr):
        remote(x_ref, block((r - d + nr) % nr, c), zs.at[d - 1], zr.at[d - 1], pr=(r + d) % nr).wait_recv()
    across = [
        remote(column(c), column(c), cs.at[d - 1], cr.at[d - 1], pc=((chip + d) % chips) * CORES + core)
        for d in range(1, chips)
    ]
    for copy in across:
        copy.start()
    over = [remote(column(c), column(c), ps.at[0], pr_.at[0], pc=partner)]
    over[0].start()
    for d in range(1, chips):
        j = ((chip - d + chips) % chips) * CORES + core
        remote(column(j), column(j), cs.at[d - 1], cr.at[d - 1], pc=partner).wait_recv()
        copy = remote(column(j), column(j), ps.at[d], pr_.at[d], pc=partner)
        copy.start()
        over.append(copy)
    for d in range(chips):
        j = ((chip - d + chips) % chips) * CORES + 1 - core
        remote(column(j), column(j), ps.at[d], pr_.at[d], pc=partner).wait_recv()
    for copy in along + across + over:
        copy.wait_send()


def gather(nr, nc, x):
    rows, cols = x.shape
    chips = nc // CORES
    flat = cols % 128 == 0
    shape = (nr * rows, nc * cols) if flat else (nc, nr * rows, cols)
    dma = pltpu.SemaphoreType.DMA
    full = pl.pallas_call(
        functools.partial(gather_kernel, nr, nc, flat),
        out_shape=jax.ShapeDtypeStruct(shape, x.dtype),
        in_specs=[pl.BlockSpec(memory_space=pltpu.VMEM)],
        out_specs=pl.BlockSpec(memory_space=pltpu.VMEM),
        scratch_shapes=[
            dma, dma((nr,)), dma((nr,)), dma((chips,)), dma((chips,)), dma((chips,)), dma((chips,)),
        ],
        compiler_params=pltpu.CompilerParams(collective_id=0, has_side_effects=True),
        name="gather",
    )(x)
    return full if flat else full.transpose(1, 0, 2).reshape(nr * rows, nc * cols)


def field_kernel(it_ref, virt_ref, occ_ref, screen_ref, out_ref, occ_t, half, back, total):
    n, m = pl.program_id(0), pl.program_id(1)
    last_n, last_m = pl.num_programs(0) - 1, pl.num_programs(1) - 1
    f32, bf16 = jnp.float32, jnp.bfloat16

    @pl.when(m == 0)
    def _():
        half[...] = jnp.dot(it_ref[...], virt_ref[...], preferred_element_type=f32).astype(bf16)
        back[...] = jnp.zeros_like(back)

    @pl.when((m == 0) & (n == 0))
    def _():
        total[...] = jnp.zeros_like(total)

    def work(turned):
        pair = jnp.dot(turned, half[...], preferred_element_type=f32)
        screened = (screen_ref[...].astype(f32) * pair).astype(bf16)
        back[...] += jnp.dot(occ_ref[...], screened, preferred_element_type=f32)

    @pl.when(n == 0)
    def _():
        turned = occ_ref[...].T
        occ_t[m] = turned
        work(turned)

    @pl.when(n != 0)
    def _():
        work(occ_t[m])

    @pl.when(m == last_m)
    def _():
        total[...] += lax.dot_general(
            back[...].astype(bf16), virt_ref[...], (((1,), (1,)), ((), ())), preferred_element_type=f32
        )

    @pl.when((m == last_m) & (n == last_n))
    def _():
        if len(out_ref.shape) == 3:
            parts, _, cols = out_ref.shape
            for q in range(parts):
                out_ref[q] = total[:, q * cols : (q + 1) * cols]
        else:
            out_ref[...] = total[...]


def field(nc, full, occ, virt, screening):
    no, nv = full.shape
    rows, cols = screening.shape
    tm, tn = min(2048, rows), min(1024, cols)
    wide = nv // nc
    shape = (nc, no, wide) if wide % 128 == 0 else (no, nv)
    out = pl.pallas_call(
        field_kernel,
        out_shape=jax.ShapeDtypeStruct(shape, jnp.float32),
        grid=(cols // tn, rows // tm),
        in_specs=[
            pl.BlockSpec((no, nv), lambda n, m: (0, 0)),
            pl.BlockSpec((nv, tn), lambda n, m: (0, n)),
            pl.BlockSpec((no, tm), lambda n, m: (0, m)),
            pl.BlockSpec((tm, tn), lambda n, m: (m, n)),
        ],
        out_specs=pl.BlockSpec(shape, lambda n, m: (0,) * len(shape)),
        scratch_shapes=[
            pltpu.VMEM((rows // tm, tm, no), jnp.bfloat16),
            pltpu.VMEM((no, tn), jnp.bfloat16),
            pltpu.VMEM((no, tn), jnp.float32),
            pltpu.VMEM((no, nv), jnp.float32),
        ],
        compiler_params=pltpu.CompilerParams(
            dimension_semantics=("arbitrary", "arbitrary"), vmem_limit_bytes=63 << 20
        ),
        name="field",
    )(full, virt, occ, screening)
    return out if wide % 128 == 0 else out.reshape(no, nc, wide).transpose(1, 0, 2)


def reduce_kernel(
    nr, nc, terms_ref, it_ref, prev_ref, side_ref, gap_ref, out_ref,
    send_a, recv_a, send_b, recv_b, send_c, recv_c, kept, own, sa, ra, sb, rb, sc, rc,
):
    r, c, chip, core, chips = place(nr, nc)
    rows, cols = it_ref.shape
    partner = chip * CORES + 1 - core
    f32, bf16 = jnp.float32, jnp.bfloat16
    greet(nr, nc)
    sends = []
    order = [*range(1, chips), 0]
    for d in order:
        k = (chip + d) % chips
        send_a[d] = terms_ref[k * CORES + 1 - core].astype(bf16)
        copy = remote(send_a.at[d], recv_a.at[d], sa.at[d], ra.at[d], pc=partner)
        copy.start()
        sends.append(copy)
    for d in order:
        k = (chip + d) % chips
        remote(send_a.at[d], recv_a.at[d], sa.at[d], ra.at[d], pc=partner).wait_recv()
        summed = terms_ref[k * CORES + core] + recv_a[d].astype(f32)
        if d:
            send_b[d] = summed.astype(bf16)
            copy = remote(send_b.at[d], recv_b.at[d], sb.at[d], rb.at[d], pc=k * CORES + core)
            copy.start()
            sends.append(copy)
        else:
            kept[...] = summed
    for d in range(1, chips):
        peer = ((chip + d) % chips) * CORES + core
        remote(send_b.at[d], recv_b.at[d], sb.at[d], rb.at[d], pc=peer).wait_recv()
        kept[...] += recv_b[d].astype(f32)
    for d in range(1, nr):
        i = (r + d) % nr
        send_c[d] = kept[pl.ds(pl.multiple_of(i * rows, rows), rows)].astype(bf16)
        copy = remote(send_c.at[d], recv_c.at[d], sc.at[d], rc.at[d], pr=i)
        copy.start()
        sends.append(copy)
    own[...] = kept[pl.ds(pl.multiple_of(r * rows, rows), rows)]
    for d in range(1, nr):
        remote(send_c.at[d], recv_c.at[d], sc.at[d], rc.at[d], pr=(r + d) % nr).wait_recv()
        own[...] += recv_c[d].astype(f32)
    current = it_ref[...].astype(f32)
    residual = side_ref[...] - gap_ref[...] * current - own[...]
    out_ref[...] = (
        current
        + relax_weight * residual / gap_ref[...]
        + momentum * (current - prev_ref[...].astype(f32))
    )
    for copy in sends:
        copy.wait_send()


def reduce_update(nr, nc, terms, iterate, previous, right_side, energy_gap):
    rows, cols = iterate.shape
    no, chips = terms.shape[1], nc // CORES
    dma, bf16, f32 = pltpu.SemaphoreType.DMA, jnp.bfloat16, jnp.float32
    return pl.pallas_call(
        functools.partial(reduce_kernel, nr, nc),
        out_shape=jax.ShapeDtypeStruct((rows, cols), f32),
        in_specs=[pl.BlockSpec(memory_space=pltpu.VMEM)] * 5,
        out_specs=pl.BlockSpec(memory_space=pltpu.VMEM),
        scratch_shapes=[
            *[pltpu.VMEM((chips, no, cols), bf16)] * 4,
            *[pltpu.VMEM((nr, rows, cols), bf16)] * 2,
            pltpu.VMEM((no, cols), f32),
            pltpu.VMEM((rows, cols), f32),
            *[dma((chips,))] * 4,
            *[dma((nr,))] * 2,
        ],
        compiler_params=pltpu.CompilerParams(collective_id=1, has_side_effects=True),
        name="reduce",
    )(terms, iterate, previous, right_side, energy_gap)


def across(q, d, chips):
    out, bit = 0, 1
    while bit < chips:
        out = out + bit * ((q // bit + d // bit) % 2)
        bit *= 2
    return out


def visits(chips):
    return sorted(range(1, chips), key=lambda d: -bin(d).count("1"))


def fused_kernel(
    nr, nc, tm, tn, it_ref, occ_hbm, virt_hbm, screen_hbm, out_ref,
    occ, occ_t, virt, half, acc, tiles, full, parts, core_out, core_in, plane_out, plane_in, line_out, line_in, kept,
    load, tile_sem, own_sem, zs, zr, cs, cr, ps, pr_, sa, ra, sb, rb, sc, rc,
):
    r, c, chip, core, chips = place(nr, nc)
    rows, cols = it_ref.shape
    no = nr * rows
    wide = CORES * cols
    steps_m, steps_n = occ_hbm.shape[1] // tm, virt_hbm.shape[1] // tn
    f32, bf16 = jnp.float32, jnp.bfloat16
    partner = chip * CORES + 1 - core
    order = visits(chips)
    sub = min(512, tm)

    def chip_at(d):
        return across(chip, d, chips)

    def tile_copy(s):
        n, m = s // steps_m, s % steps_m
        source = screen_hbm.at[
            pl.ds(pl.multiple_of(m * tm, tm), tm), pl.ds(pl.multiple_of(n * tn, tn), tn)
        ]
        return pltpu.make_async_copy(source, tiles.at[s % 2], tile_sem.at[s % 2])

    def block(i, q, k):
        return full.at[
            q, pl.ds(pl.multiple_of(i * rows, rows), rows), pl.ds(pl.multiple_of(k * cols, cols), cols)
        ]

    occ_load = pltpu.make_async_copy(occ_hbm, occ, load.at[0])
    virt_load = pltpu.make_async_copy(virt_hbm, virt, load.at[1])
    occ_load.start()
    virt_load.start()
    tile_copy(0).start()
    greet(nr, nc)

    own = pltpu.make_async_copy(it_ref, block(r, chip, core), own_sem)
    own.start()
    sends = []

    def start(copy):
        copy.start()
        sends.append(copy)

    for d in range(1, nr):
        start(remote(it_ref, block(r, chip, core), zs.at[d], zr.at[d], pr=(r + d) % nr))

    def spread(e, source, i):
        for d in order:
            start(remote(
                source, block(i, chip, core), cs.at[d, e], cr.at[d, e], pc=chip_at(d) * CORES + core
            ))
        start(remote(source, block(i, chip, core), ps.at[0, e], pr_.at[0, e], pc=partner))

    spread(0, it_ref, r)

    occ_load.wait()
    turn = min(512, tm)

    @pl.loop(0, occ_hbm.shape[1] // turn)
    def _(j):
        at = pl.ds(pl.multiple_of(j * turn, turn), turn)
        occ_t[at] = occ[:, at].T

    for e in range(1, nr):
        i = (r - e + nr) % nr
        here = block(i, chip, core)
        remote(it_ref, here, zs.at[e], zr.at[e], pr=(r + e) % nr).wait_recv()
        spread(e, here, i)
    own.wait()
    virt_load.wait()

    def arrive(d, from_core):
        q = chip_at(d)
        for e in range(nr):
            i = (r - e + nr) % nr
            if from_core:
                there = block(i, q, 1 - core)
                remote(there, there, ps.at[d, e], pr_.at[d, e], pc=partner).wait_recv()
            else:
                here = block(i, q, core)
                remote(here, here, cs.at[d, e], cr.at[d, e], pc=q * CORES + core).wait_recv()
                start(remote(here, here, ps.at[d, e], pr_.at[d, e], pc=partner))

    def project(d):
        q = chip_at(d)
        return jnp.dot(
            full[q], virt[pl.ds(pl.multiple_of(q * wide, wide), wide), :], preferred_element_type=f32
        )

    queue = [0, *order[::-1]]
    for p, d in enumerate(queue):
        if d:
            arrive(d, False)
        arrive(d, True)
        if len(queue) == 1:
            half[...] = project(d).astype(bf16)
        elif p == 0:
            acc[...] = project(d)
        elif p < len(queue) - 1:
            acc[...] += project(d)
        else:
            half[...] = (acc[...] + project(d)).astype(bf16)

    @pl.loop(0, steps_n * steps_m)
    def _(s):
        n, m = s // steps_m, s % steps_m
        tile_copy(s).wait()

        @pl.when(s + 1 < steps_n * steps_m)
        def _():
            tile_copy(s + 1).start()

        at_n = pl.ds(pl.multiple_of(n * tn, tn), tn)
        at_m = pl.ds(pl.multiple_of(m * tm, tm), tm)
        tile = tiles.at[s % 2]
        for j in range(0, tm, sub):
            turned = occ_t[pl.ds(pl.multiple_of(m * tm + j, sub), sub)]
            pair = jnp.dot(turned, half[:, at_n], preferred_element_type=f32)
            tile[j : j + sub] = (tile[j : j + sub].astype(f32) * pair).astype(bf16)
        back = jnp.dot(occ[:, at_m], tile[...], preferred_element_type=f32)
        acc[:, at_n] = jnp.where(m == 0, 0.0, acc[:, at_n]) + back

        @pl.when(m == steps_m - 1)
        def _():
            half[:, at_n] = acc[:, at_n].astype(bf16)

    def fold(d):
        copy = remote(core_out.at[d], core_in.at[d], sa.at[d], ra.at[d], pc=partner)
        copy.wait_recv()
        summed = parts[d, core] + core_in[d].astype(f32)
        if d:
            plane_out[d] = summed.astype(bf16)
            start(remote(
                plane_out.at[d], plane_in.at[d], sb.at[d], rb.at[d], pc=chip_at(d) * CORES + core
            ))
        else:
            kept[...] = summed

    before = None
    for d in [*order, 0]:
        q = chip_at(d)
        product = lax.dot_general(
            half[...], virt[pl.ds(pl.multiple_of(q * wide, wide), wide), :], (((1,), (1,)), ((), ())),
            preferred_element_type=f32,
        )
        for k in range(CORES):
            parts[d, k] = product[:, k * cols : (k + 1) * cols]
        core_out[d] = parts[d, 1 - core].astype(bf16)
        start(remote(core_out.at[d], core_in.at[d], sa.at[d], ra.at[d], pc=partner))
        if before is not None:
            fold(before)
        before = d
    fold(0)
    for d in order:
        remote(
            plane_out.at[d], plane_in.at[d], sb.at[d], rb.at[d], pc=chip_at(d) * CORES + core
        ).wait_recv()
        kept[...] += plane_in[d].astype(f32)
    for d in range(1, nr):
        i = (r + d) % nr
        line_out[d] = kept[pl.ds(pl.multiple_of(i * rows, rows), rows)].astype(bf16)
        start(remote(line_out.at[d], line_in.at[d], sc.at[d], rc.at[d], pr=i))
    total = kept[pl.ds(pl.multiple_of(r * rows, rows), rows)]
    for d in range(1, nr):
        remote(line_out.at[d], line_in.at[d], sc.at[d], rc.at[d], pr=(r + d) % nr).wait_recv()
        total = total + line_in[d].astype(f32)
    out_ref[...] = total
    for copy in sends:
        copy.wait_send()


def fused(nr, nc, iterate, occ, virt, screening):
    rows, cols = iterate.shape
    no, nv, chips = nr * rows, nc * cols, nc // CORES
    tall, long = screening.shape
    tm, tn = min(2048, tall), min(1024, long)
    dma, bf16, f32 = pltpu.SemaphoreType.DMA, jnp.bfloat16, jnp.float32
    vmem = pltpu.VMEM
    return pl.pallas_call(
        functools.partial(fused_kernel, nr, nc, tm, tn),
        out_shape=jax.ShapeDtypeStruct((rows, cols), f32),
        in_specs=[pl.BlockSpec(memory_space=pltpu.VMEM)] + [pl.BlockSpec(memory_space=pl.ANY)] * 3,
        out_specs=pl.BlockSpec(memory_space=pltpu.VMEM),
        scratch_shapes=[
            vmem((no, tall), bf16),
            vmem((tall, no), bf16),
            vmem((nv, long), bf16),
            vmem((no, long), bf16),
            vmem((no, long), f32),
            vmem((2, tm, tn), bf16),
            vmem((chips, no, CORES * cols), bf16),
            vmem((chips, CORES, no, cols), f32),
            *[vmem((chips, no, cols), bf16)] * 4,
            *[vmem((nr, rows, cols), bf16)] * 2,
            vmem((no, cols), f32),
            dma((2,)),
            dma((2,)),
            dma,
            *[dma((nr,))] * 2,
            *[dma((chips, nr))] * 4,
            *[dma((chips,))] * 4,
            *[dma((nr,))] * 2,
        ],
        compiler_params=pltpu.CompilerParams(
            collective_id=0, has_side_effects=True, vmem_limit_bytes=63 << 20
        ),
        name="fused",
    )(iterate, occ, virt, screening)


def fits(nr, nc, iterate, screening):
    rows, cols = iterate.shape
    chips = nc // CORES
    return nc % CORES == 0 and chips & (chips - 1) == 0 and rows % 16 == 0 and cols % 128 == 0


def solution(mesh):
    nr, nc = mesh.shape["pr"], mesh.shape["pc"]

    def on_device(iterate, previous, right_side, energy_gap, occ_points, virt_points, screening):
        if fits(nr, nc, iterate, screening):
            kernel = fused(nr, nc, iterate, occ_points, virt_points, screening)
            current = iterate.astype(jnp.float32)
            residual = right_side - energy_gap * current - kernel
            return (
                current
                + relax_weight * residual / energy_gap
                + momentum * (current - previous.astype(jnp.float32))
            )
        full = gather(nr, nc, iterate)
        terms = field(nc, full, occ_points, virt_points, screening)
        return reduce_update(nr, nc, terms, iterate, previous, right_side, energy_gap)

    return jax.shard_map(
        on_device,
        mesh=mesh,
        in_specs=(
            P("pr", "pc"),
            P("pr", "pc"),
            P("pr", "pc"),
            P("pr", "pc"),
            P(None, "pr"),
            P(None, "pc"),
            P("pr", "pc"),
        ),
        out_specs=P("pr", "pc"),
        check_vma=False,
    )
```

```python
import functools

import jax
import jax.numpy as jnp
from jax import lax
from jax.experimental import pallas as pl
from jax.experimental.pallas import tpu as pltpu
from jax.sharding import PartitionSpec as P

relax_weight = 0.8
momentum = 0.3
MESH = pl.DeviceIdType.MESH
CORES = 2


def place(nr, nc):
    r, c = lax.axis_index("pr"), lax.axis_index("pc")
    chips = nc // CORES
    return r, c, c // CORES, c % CORES, chips


def greet(nr, nc):
    r, c, chip, core, chips = place(nr, nc)
    barrier = pltpu.get_barrier_semaphore()
    for d in range(1, nr):
        pl.semaphore_signal(barrier, inc=1, device_id={"pr": (r + d) % nr}, device_id_type=MESH)
    for d in range(1, chips):
        peer = ((chip + d) % chips) * CORES + core
        pl.semaphore_signal(barrier, inc=1, device_id={"pc": peer}, device_id_type=MESH)
    pl.semaphore_signal(barrier, inc=1, device_id={"pc": chip * CORES + 1 - core}, device_id_type=MESH)
    pl.semaphore_wait(barrier, nr - 1 + chips)


def remote(src, dst, send, recv, **where):
    return pltpu.make_async_remote_copy(
        src_ref=src, dst_ref=dst, send_sem=send, recv_sem=recv, device_id=where, device_id_type=MESH
    )


def gather_kernel(nr, nc, flat, x_ref, out_ref, own_sem, zs, zr, cs, cr, ps, pr_):
    r, c, chip, core, chips = place(nr, nc)
    rows, cols = x_ref.shape
    partner = chip * CORES + 1 - core

    def column(j):
        if flat:
            return out_ref.at[:, pl.ds(pl.multiple_of(j * cols, cols), cols)]
        return out_ref.at[j]

    def block(i, j):
        own = pl.ds(pl.multiple_of(i * rows, rows), rows)
        if flat:
            return out_ref.at[own, pl.ds(pl.multiple_of(j * cols, cols), cols)]
        return out_ref.at[j, own]

    greet(nr, nc)
    keep = pltpu.make_async_copy(x_ref, block(r, c), own_sem)
    keep.start()
    along = [
        remote(x_ref, block(r, c), zs.at[d - 1], zr.at[d - 1], pr=(r + d) % nr) for d in range(1, nr)
    ]
    for copy in along:
        copy.start()
    keep.wait()
    for d in range(1, nr):
        remote(x_ref, block((r - d + nr) % nr, c), zs.at[d - 1], zr.at[d - 1], pr=(r + d) % nr).wait_recv()
    across = [
        remote(column(c), column(c), cs.at[d - 1], cr.at[d - 1], pc=((chip + d) % chips) * CORES + core)
        for d in range(1, chips)
    ]
    for copy in across:
        copy.start()
    over = [remote(column(c), column(c), ps.at[0], pr_.at[0], pc=partner)]
    over[0].start()
    for d in range(1, chips):
        j = ((chip - d + chips) % chips) * CORES + core
        remote(column(j), column(j), cs.at[d - 1], cr.at[d - 1], pc=partner).wait_recv()
        copy = remote(column(j), column(j), ps.at[d], pr_.at[d], pc=partner)
        copy.start()
        over.append(copy)
    for d in range(chips):
        j = ((chip - d + chips) % chips) * CORES + 1 - core
        remote(column(j), column(j), ps.at[d], pr_.at[d], pc=partner).wait_recv()
    for copy in along + across + over:
        copy.wait_send()


def gather(nr, nc, x):
    rows, cols = x.shape
    chips = nc // CORES
    flat = cols % 128 == 0
    shape = (nr * rows, nc * cols) if flat else (nc, nr * rows, cols)
    dma = pltpu.SemaphoreType.DMA
    full = pl.pallas_call(
        functools.partial(gather_kernel, nr, nc, flat),
        out_shape=jax.ShapeDtypeStruct(shape, x.dtype),
        in_specs=[pl.BlockSpec(memory_space=pltpu.VMEM)],
        out_specs=pl.BlockSpec(memory_space=pltpu.VMEM),
        scratch_shapes=[
            dma, dma((nr,)), dma((nr,)), dma((chips,)), dma((chips,)), dma((chips,)), dma((chips,)),
        ],
        compiler_params=pltpu.CompilerParams(collective_id=0, has_side_effects=True),
        name="gather",
    )(x)
    return full if flat else full.transpose(1, 0, 2).reshape(nr * rows, nc * cols)


def field_kernel(it_ref, virt_ref, occ_ref, screen_ref, out_ref, occ_t, half, back, total):
    n, m = pl.program_id(0), pl.program_id(1)
    last_n, last_m = pl.num_programs(0) - 1, pl.num_programs(1) - 1
    f32, bf16 = jnp.float32, jnp.bfloat16

    @pl.when(m == 0)
    def _():
        half[...] = jnp.dot(it_ref[...], virt_ref[...], preferred_element_type=f32).astype(bf16)
        back[...] = jnp.zeros_like(back)

    @pl.when((m == 0) & (n == 0))
    def _():
        total[...] = jnp.zeros_like(total)

    def work(turned):
        pair = jnp.dot(turned, half[...], preferred_element_type=f32)
        screened = (screen_ref[...].astype(f32) * pair).astype(bf16)
        back[...] += jnp.dot(occ_ref[...], screened, preferred_element_type=f32)

    @pl.when(n == 0)
    def _():
        turned = occ_ref[...].T
        occ_t[m] = turned
        work(turned)

    @pl.when(n != 0)
    def _():
        work(occ_t[m])

    @pl.when(m == last_m)
    def _():
        total[...] += lax.dot_general(
            back[...].astype(bf16), virt_ref[...], (((1,), (1,)), ((), ())), preferred_element_type=f32
        )

    @pl.when((m == last_m) & (n == last_n))
    def _():
        if len(out_ref.shape) == 3:
            parts, _, cols = out_ref.shape
            for q in range(parts):
                out_ref[q] = total[:, q * cols : (q + 1) * cols]
        else:
            out_ref[...] = total[...]


def field(nc, full, occ, virt, screening):
    no, nv = full.shape
    rows, cols = screening.shape
    tm, tn = min(2048, rows), min(1024, cols)
    wide = nv // nc
    shape = (nc, no, wide) if wide % 128 == 0 else (no, nv)
    out = pl.pallas_call(
        field_kernel,
        out_shape=jax.ShapeDtypeStruct(shape, jnp.float32),
        grid=(cols // tn, rows // tm),
        in_specs=[
            pl.BlockSpec((no, nv), lambda n, m: (0, 0)),
            pl.BlockSpec((nv, tn), lambda n, m: (0, n)),
            pl.BlockSpec((no, tm), lambda n, m: (0, m)),
            pl.BlockSpec((tm, tn), lambda n, m: (m, n)),
        ],
        out_specs=pl.BlockSpec(shape, lambda n, m: (0,) * len(shape)),
        scratch_shapes=[
            pltpu.VMEM((rows // tm, tm, no), jnp.bfloat16),
            pltpu.VMEM((no, tn), jnp.bfloat16),
            pltpu.VMEM((no, tn), jnp.float32),
            pltpu.VMEM((no, nv), jnp.float32),
        ],
        compiler_params=pltpu.CompilerParams(
            dimension_semantics=("arbitrary", "arbitrary"), vmem_limit_bytes=63 << 20
        ),
        name="field",
    )(full, virt, occ, screening)
    return out if wide % 128 == 0 else out.reshape(no, nc, wide).transpose(1, 0, 2)


def reduce_kernel(
    nr, nc, terms_ref, it_ref, prev_ref, side_ref, gap_ref, out_ref,
    send_a, recv_a, send_b, recv_b, send_c, recv_c, kept, own, sa, ra, sb, rb, sc, rc,
):
    r, c, chip, core, chips = place(nr, nc)
    rows, cols = it_ref.shape
    partner = chip * CORES + 1 - core
    f32, bf16 = jnp.float32, jnp.bfloat16
    greet(nr, nc)
    sends = []
    order = [*range(1, chips), 0]
    for d in order:
        k = (chip + d) % chips
        send_a[d] = terms_ref[k * CORES + 1 - core].astype(bf16)
        copy = remote(send_a.at[d], recv_a.at[d], sa.at[d], ra.at[d], pc=partner)
        copy.start()
        sends.append(copy)
    for d in order:
        k = (chip + d) % chips
        remote(send_a.at[d], recv_a.at[d], sa.at[d], ra.at[d], pc=partner).wait_recv()
        summed = terms_ref[k * CORES + core] + recv_a[d].astype(f32)
        if d:
            send_b[d] = summed.astype(bf16)
            copy = remote(send_b.at[d], recv_b.at[d], sb.at[d], rb.at[d], pc=k * CORES + core)
            copy.start()
            sends.append(copy)
        else:
            kept[...] = summed
    for d in range(1, chips):
        peer = ((chip + d) % chips) * CORES + core
        remote(send_b.at[d], recv_b.at[d], sb.at[d], rb.at[d], pc=peer).wait_recv()
        kept[...] += recv_b[d].astype(f32)
    for d in range(1, nr):
        i = (r + d) % nr
        send_c[d] = kept[pl.ds(pl.multiple_of(i * rows, rows), rows)].astype(bf16)
        copy = remote(send_c.at[d], recv_c.at[d], sc.at[d], rc.at[d], pr=i)
        copy.start()
        sends.append(copy)
    own[...] = kept[pl.ds(pl.multiple_of(r * rows, rows), rows)]
    for d in range(1, nr):
        remote(send_c.at[d], recv_c.at[d], sc.at[d], rc.at[d], pr=(r + d) % nr).wait_recv()
        own[...] += recv_c[d].astype(f32)
    current = it_ref[...].astype(f32)
    residual = side_ref[...] - gap_ref[...] * current - own[...]
    out_ref[...] = (
        current
        + relax_weight * residual / gap_ref[...]
        + momentum * (current - prev_ref[...].astype(f32))
    )
    for copy in sends:
        copy.wait_send()


def reduce_update(nr, nc, terms, iterate, previous, right_side, energy_gap):
    rows, cols = iterate.shape
    no, chips = terms.shape[1], nc // CORES
    dma, bf16, f32 = pltpu.SemaphoreType.DMA, jnp.bfloat16, jnp.float32
    return pl.pallas_call(
        functools.partial(reduce_kernel, nr, nc),
        out_shape=jax.ShapeDtypeStruct((rows, cols), f32),
        in_specs=[pl.BlockSpec(memory_space=pltpu.VMEM)] * 5,
        out_specs=pl.BlockSpec(memory_space=pltpu.VMEM),
        scratch_shapes=[
            *[pltpu.VMEM((chips, no, cols), bf16)] * 4,
            *[pltpu.VMEM((nr, rows, cols), bf16)] * 2,
            pltpu.VMEM((no, cols), f32),
            pltpu.VMEM((rows, cols), f32),
            *[dma((chips,))] * 4,
            *[dma((nr,))] * 2,
        ],
        compiler_params=pltpu.CompilerParams(collective_id=1, has_side_effects=True),
        name="reduce",
    )(terms, iterate, previous, right_side, energy_gap)


def across(q, d, chips):
    out, bit = 0, 1
    while bit < chips:
        out = out + bit * ((q // bit + d // bit) % 2)
        bit *= 2
    return out


def visits(chips):
    return sorted(range(1, chips), key=lambda d: -bin(d).count("1"))


def fused_kernel(
    nr, nc, tm, tn, it_ref, occ_hbm, virt_hbm, screen_hbm, out_ref,
    occ, occ_t, virt, half, acc, tiles, full, parts, core_out, core_in, plane_out, plane_in, line_out, line_in, kept,
    load, tile_sem, own_sem, zs, zr, cs, cr, ps, pr_, sa, ra, sb, rb, sc, rc,
):
    r, c, chip, core, chips = place(nr, nc)
    rows, cols = it_ref.shape
    no = nr * rows
    wide = CORES * cols
    steps_m, steps_n = occ_hbm.shape[1] // tm, virt_hbm.shape[1] // tn
    f32, bf16 = jnp.float32, jnp.bfloat16
    partner = chip * CORES + 1 - core
    order = visits(chips)
    sub = min(512, tm)

    def chip_at(d):
        return across(chip, d, chips)

    def tile_copy(s):
        n, m = s // steps_m, s % steps_m
        source = screen_hbm.at[
            pl.ds(pl.multiple_of(m * tm, tm), tm), pl.ds(pl.multiple_of(n * tn, tn), tn)
        ]
        return pltpu.make_async_copy(source, tiles.at[s % 2], tile_sem.at[s % 2])

    def block(i, q, k):
        return full.at[
            q, pl.ds(pl.multiple_of(i * rows, rows), rows), pl.ds(pl.multiple_of(k * cols, cols), cols)
        ]

    occ_load = pltpu.make_async_copy(occ_hbm, occ, load.at[0])
    virt_load = pltpu.make_async_copy(virt_hbm, virt, load.at[1])
    occ_load.start()
    virt_load.start()
    tile_copy(0).start()
    greet(nr, nc)

    own = pltpu.make_async_copy(it_ref, block(r, chip, core), own_sem)
    own.start()
    sends = []

    def start(copy):
        copy.start()
        sends.append(copy)

    for d in range(1, nr):
        start(remote(it_ref, block(r, chip, core), zs.at[d], zr.at[d], pr=(r + d) % nr))

    def spread(e, source, i):
        for d in order:
            start(remote(
                source, block(i, chip, core), cs.at[d, e], cr.at[d, e], pc=chip_at(d) * CORES + core
            ))
        start(remote(source, block(i, chip, core), ps.at[0, e], pr_.at[0, e], pc=partner))

    spread(0, it_ref, r)

    for e in range(1, nr):
        i = (r - e + nr) % nr
        here = block(i, chip, core)
        remote(it_ref, here, zs.at[e], zr.at[e], pr=(r + e) % nr).wait_recv()
        spread(e, here, i)
    own.wait()

    occ_load.wait()
    turn = min(512, tm)

    @pl.loop(0, occ_hbm.shape[1] // turn)
    def _(j):
        at = pl.ds(pl.multiple_of(j * turn, turn), turn)
        occ_t[at] = occ[:, at].T

    def forward(d, e):
        q = chip_at(d)
        here = block((r - e + nr) % nr, q, core)
        remote(here, here, cs.at[d, e], cr.at[d, e], pc=q * CORES + core).wait_recv()
        start(remote(here, here, ps.at[d, e], pr_.at[d, e], pc=partner))

    def project(d):
        q = chip_at(d)
        for e in range(nr):
            there = block((r - e + nr) % nr, q, 1 - core)
            remote(there, there, ps.at[d, e], pr_.at[d, e], pc=partner).wait_recv()
        at_q = pl.ds(pl.multiple_of(q * wide, wide), wide)
        for j in range(0, virt_hbm.shape[1], tn):
            at = pl.ds(j, tn)
            term = jnp.dot(full[q], virt[at_q, at], preferred_element_type=f32)
            if d == 0:
                acc[:, at] = term
            elif d == order[-1]:
                half[:, at] = (acc[:, at] + term).astype(bf16)
            else:
                acc[:, at] += term

    virt_load.wait()
    project(0)
    for e in range(nr):
        for d in order:
            forward(d, e)
    for d in order:
        project(d)

    @pl.loop(0, steps_n * steps_m)
    def _(s):
        n, m = s // steps_m, s % steps_m
        tile_copy(s).wait()

        @pl.when(s + 1 < steps_n * steps_m)
        def _():
            tile_copy(s + 1).start()

        at_n = pl.ds(pl.multiple_of(n * tn, tn), tn)
        at_m = pl.ds(pl.multiple_of(m * tm, tm), tm)
        tile = tiles.at[s % 2]
        for j in range(0, tm, sub):
            turned = occ_t[pl.ds(pl.multiple_of(m * tm + j, sub), sub)]
            pair = jnp.dot(turned, half[:, at_n], preferred_element_type=f32)
            tile[j : j + sub] = (tile[j : j + sub].astype(f32) * pair).astype(bf16)
        back = jnp.dot(occ[:, at_m], tile[...], preferred_element_type=f32)
        acc[:, at_n] = jnp.where(m == 0, 0.0, acc[:, at_n]) + back

        @pl.when(m == steps_m - 1)
        def _():
            half[:, at_n] = acc[:, at_n].astype(bf16)

    bands = 2 if nr % 2 == 0 else 1
    tall = no // bands

    def band(ref, d, h):
        return ref.at[d, pl.ds(h * tall, tall)]

    def to_partner(d, h):
        return remote(band(core_out, d, h), band(core_in, d, h), sa.at[d, h], ra.at[d, h], pc=partner)

    def to_chip(d, h):
        return remote(
            band(plane_out, d, h), band(plane_in, d, h), sb.at[d, h], rb.at[d, h],
            pc=chip_at(d) * CORES + core,
        )

    def along(d):
        return remote(line_out.at[d], line_in.at[d], sc.at[d], rc.at[d], pr=(r + d) % nr)

    def fold(h, d):
        at = pl.ds(h * tall, tall)
        to_partner(d, h).wait_recv()
        summed = parts[d, core, at] + core_in[d, at].astype(f32)
        if d:
            plane_out[d, at] = summed.astype(bf16)
            start(to_chip(d, h))
        else:
            kept[at] = summed

    pieces = [(h, d) for h in range(bands) for d in [*order, 0]]
    for p, (h, d) in enumerate(pieces):
        q = chip_at(d)
        product = lax.dot_general(
            half[h * tall : (h + 1) * tall], virt[pl.ds(pl.multiple_of(q * wide, wide), wide), :],
            (((1,), (1,)), ((), ())), preferred_element_type=f32,
        )
        at = pl.ds(h * tall, tall)
        for k in range(CORES):
            parts[d, k, at] = product[:, k * cols : (k + 1) * cols]
        core_out[d, at] = parts[d, 1 - core, at].astype(bf16)
        start(to_partner(d, h))
        if p >= 1:
            fold(*pieces[p - 1])
    for piece in pieces[-1:]:
        fold(*piece)
    for h in range(bands):
        at = pl.ds(h * tall, tall)
        for d in order:
            to_chip(d, h).wait_recv()
            kept[at] += plane_in[d, at].astype(f32)
        for d in range(1, nr):
            i = (r + d) % nr

            @pl.when(i // (nr // bands) == h)
            def _():
                line_out[d] = kept[pl.ds(pl.multiple_of(i * rows, rows), rows)].astype(bf16)
                along(d).start()

    total = kept[pl.ds(pl.multiple_of(r * rows, rows), rows)]
    for d in range(1, nr):
        along(d).wait_recv()
        total = total + line_in[d].astype(f32)
    out_ref[...] = total
    for d in range(1, nr):
        along(d).wait_send()
    for copy in sends:
        copy.wait_send()


def fused(nr, nc, iterate, occ, virt, screening):
    rows, cols = iterate.shape
    no, nv, chips = nr * rows, nc * cols, nc // CORES
    tall, long = screening.shape
    tm, tn = min(2048, tall), min(1024, long)
    dma, bf16, f32 = pltpu.SemaphoreType.DMA, jnp.bfloat16, jnp.float32
    vmem = pltpu.VMEM
    return pl.pallas_call(
        functools.partial(fused_kernel, nr, nc, tm, tn),
        out_shape=jax.ShapeDtypeStruct((rows, cols), f32),
        in_specs=[pl.BlockSpec(memory_space=pltpu.VMEM)] + [pl.BlockSpec(memory_space=pl.ANY)] * 3,
        out_specs=pl.BlockSpec(memory_space=pltpu.VMEM),
        scratch_shapes=[
            vmem((no, tall), bf16),
            vmem((tall, no), bf16),
            vmem((nv, long), bf16),
            vmem((no, long), bf16),
            vmem((no, long), f32),
            vmem((2, tm, tn), bf16),
            vmem((chips, no, CORES * cols), bf16),
            vmem((chips, CORES, no, cols), f32),
            *[vmem((chips, no, cols), bf16)] * 4,
            *[vmem((nr, rows, cols), bf16)] * 2,
            vmem((no, cols), f32),
            dma((2,)),
            dma((2,)),
            dma,
            *[dma((nr,))] * 2,
            *[dma((chips, nr))] * 4,
            *[dma((chips, 2))] * 4,
            *[dma((nr,))] * 2,
        ],
        compiler_params=pltpu.CompilerParams(
            collective_id=0, has_side_effects=True, vmem_limit_bytes=63 << 20
        ),
        name="fused",
    )(iterate, occ, virt, screening)


def fits(nr, nc, iterate, screening):
    rows, cols = iterate.shape
    chips = nc // CORES
    return nc % CORES == 0 and chips > 1 and chips & (chips - 1) == 0 and rows % 16 == 0 and cols % 128 == 0


def solution(mesh):
    nr, nc = mesh.shape["pr"], mesh.shape["pc"]

    def on_device(iterate, previous, right_side, energy_gap, occ_points, virt_points, screening):
        if fits(nr, nc, iterate, screening):
            kernel = fused(nr, nc, iterate, occ_points, virt_points, screening)
            current = iterate.astype(jnp.float32)
            residual = right_side - energy_gap * current - kernel
            return (
                current
                + relax_weight * residual / energy_gap
                + momentum * (current - previous.astype(jnp.float32))
            )
        full = gather(nr, nc, iterate)
        terms = field(nc, full, occ_points, virt_points, screening)
        return reduce_update(nr, nc, terms, iterate, previous, right_side, energy_gap)

    return jax.shard_map(
        on_device,
        mesh=mesh,
        in_specs=(
            P("pr", "pc"),
            P("pr", "pc"),
            P("pr", "pc"),
            P("pr", "pc"),
            P(None, "pr"),
            P(None, "pc"),
            P("pr", "pc"),
        ),
        out_specs=P("pr", "pc"),
        check_vma=False,
    )
```

```python
import functools

import jax
import jax.numpy as jnp
from jax import lax
from jax.experimental import pallas as pl
from jax.experimental.pallas import tpu as pltpu
from jax.sharding import PartitionSpec as P

relax_weight = 0.8
momentum = 0.3
MESH = pl.DeviceIdType.MESH
CORES = 2


def place(nr, nc):
    r, c = lax.axis_index("pr"), lax.axis_index("pc")
    chips = nc // CORES
    return r, c, c // CORES, c % CORES, chips


def greet(nr, nc):
    r, c, chip, core, chips = place(nr, nc)
    barrier = pltpu.get_barrier_semaphore()
    for d in range(1, nr):
        pl.semaphore_signal(barrier, inc=1, device_id={"pr": (r + d) % nr}, device_id_type=MESH)
    for d in range(1, chips):
        peer = ((chip + d) % chips) * CORES + core
        pl.semaphore_signal(barrier, inc=1, device_id={"pc": peer}, device_id_type=MESH)
    pl.semaphore_signal(barrier, inc=1, device_id={"pc": chip * CORES + 1 - core}, device_id_type=MESH)
    pl.semaphore_wait(barrier, nr - 1 + chips)


def remote(src, dst, send, recv, **where):
    return pltpu.make_async_remote_copy(
        src_ref=src, dst_ref=dst, send_sem=send, recv_sem=recv, device_id=where, device_id_type=MESH
    )


def gather_kernel(nr, nc, flat, x_ref, out_ref, own_sem, zs, zr, cs, cr, ps, pr_):
    r, c, chip, core, chips = place(nr, nc)
    rows, cols = x_ref.shape
    partner = chip * CORES + 1 - core

    def column(j):
        if flat:
            return out_ref.at[:, pl.ds(pl.multiple_of(j * cols, cols), cols)]
        return out_ref.at[j]

    def block(i, j):
        own = pl.ds(pl.multiple_of(i * rows, rows), rows)
        if flat:
            return out_ref.at[own, pl.ds(pl.multiple_of(j * cols, cols), cols)]
        return out_ref.at[j, own]

    greet(nr, nc)
    keep = pltpu.make_async_copy(x_ref, block(r, c), own_sem)
    keep.start()
    along = [
        remote(x_ref, block(r, c), zs.at[d - 1], zr.at[d - 1], pr=(r + d) % nr) for d in range(1, nr)
    ]
    for copy in along:
        copy.start()
    keep.wait()
    for d in range(1, nr):
        remote(x_ref, block((r - d + nr) % nr, c), zs.at[d - 1], zr.at[d - 1], pr=(r + d) % nr).wait_recv()
    across = [
        remote(column(c), column(c), cs.at[d - 1], cr.at[d - 1], pc=((chip + d) % chips) * CORES + core)
        for d in range(1, chips)
    ]
    for copy in across:
        copy.start()
    over = [remote(column(c), column(c), ps.at[0], pr_.at[0], pc=partner)]
    over[0].start()
    for d in range(1, chips):
        j = ((chip - d + chips) % chips) * CORES + core
        remote(column(j), column(j), cs.at[d - 1], cr.at[d - 1], pc=partner).wait_recv()
        copy = remote(column(j), column(j), ps.at[d], pr_.at[d], pc=partner)
        copy.start()
        over.append(copy)
    for d in range(chips):
        j = ((chip - d + chips) % chips) * CORES + 1 - core
        remote(column(j), column(j), ps.at[d], pr_.at[d], pc=partner).wait_recv()
    for copy in along + across + over:
        copy.wait_send()


def gather(nr, nc, x):
    rows, cols = x.shape
    chips = nc // CORES
    flat = cols % 128 == 0
    shape = (nr * rows, nc * cols) if flat else (nc, nr * rows, cols)
    dma = pltpu.SemaphoreType.DMA
    full = pl.pallas_call(
        functools.partial(gather_kernel, nr, nc, flat),
        out_shape=jax.ShapeDtypeStruct(shape, x.dtype),
        in_specs=[pl.BlockSpec(memory_space=pltpu.VMEM)],
        out_specs=pl.BlockSpec(memory_space=pltpu.VMEM),
        scratch_shapes=[
            dma, dma((nr,)), dma((nr,)), dma((chips,)), dma((chips,)), dma((chips,)), dma((chips,)),
        ],
        compiler_params=pltpu.CompilerParams(collective_id=0, has_side_effects=True),
        name="gather",
    )(x)
    return full if flat else full.transpose(1, 0, 2).reshape(nr * rows, nc * cols)


def field_kernel(it_ref, virt_ref, occ_ref, screen_ref, out_ref, occ_t, half, back, total):
    n, m = pl.program_id(0), pl.program_id(1)
    last_n, last_m = pl.num_programs(0) - 1, pl.num_programs(1) - 1
    f32, bf16 = jnp.float32, jnp.bfloat16

    @pl.when(m == 0)
    def _():
        half[...] = jnp.dot(it_ref[...], virt_ref[...], preferred_element_type=f32).astype(bf16)
        back[...] = jnp.zeros_like(back)

    @pl.when((m == 0) & (n == 0))
    def _():
        total[...] = jnp.zeros_like(total)

    def work(turned):
        pair = jnp.dot(turned, half[...], preferred_element_type=f32)
        screened = (screen_ref[...].astype(f32) * pair).astype(bf16)
        back[...] += jnp.dot(occ_ref[...], screened, preferred_element_type=f32)

    @pl.when(n == 0)
    def _():
        turned = occ_ref[...].T
        occ_t[m] = turned
        work(turned)

    @pl.when(n != 0)
    def _():
        work(occ_t[m])

    @pl.when(m == last_m)
    def _():
        total[...] += lax.dot_general(
            back[...].astype(bf16), virt_ref[...], (((1,), (1,)), ((), ())), preferred_element_type=f32
        )

    @pl.when((m == last_m) & (n == last_n))
    def _():
        if len(out_ref.shape) == 3:
            parts, _, cols = out_ref.shape
            for q in range(parts):
                out_ref[q] = total[:, q * cols : (q + 1) * cols]
        else:
            out_ref[...] = total[...]


def field(nc, full, occ, virt, screening):
    no, nv = full.shape
    rows, cols = screening.shape
    tm, tn = min(2048, rows), min(1024, cols)
    wide = nv // nc
    shape = (nc, no, wide) if wide % 128 == 0 else (no, nv)
    out = pl.pallas_call(
        field_kernel,
        out_shape=jax.ShapeDtypeStruct(shape, jnp.float32),
        grid=(cols // tn, rows // tm),
        in_specs=[
            pl.BlockSpec((no, nv), lambda n, m: (0, 0)),
            pl.BlockSpec((nv, tn), lambda n, m: (0, n)),
            pl.BlockSpec((no, tm), lambda n, m: (0, m)),
            pl.BlockSpec((tm, tn), lambda n, m: (m, n)),
        ],
        out_specs=pl.BlockSpec(shape, lambda n, m: (0,) * len(shape)),
        scratch_shapes=[
            pltpu.VMEM((rows // tm, tm, no), jnp.bfloat16),
            pltpu.VMEM((no, tn), jnp.bfloat16),
            pltpu.VMEM((no, tn), jnp.float32),
            pltpu.VMEM((no, nv), jnp.float32),
        ],
        compiler_params=pltpu.CompilerParams(
            dimension_semantics=("arbitrary", "arbitrary"), vmem_limit_bytes=63 << 20
        ),
        name="field",
    )(full, virt, occ, screening)
    return out if wide % 128 == 0 else out.reshape(no, nc, wide).transpose(1, 0, 2)


def reduce_kernel(
    nr, nc, terms_ref, it_ref, prev_ref, side_ref, gap_ref, out_ref,
    send_a, recv_a, send_b, recv_b, send_c, recv_c, kept, own, sa, ra, sb, rb, sc, rc,
):
    r, c, chip, core, chips = place(nr, nc)
    rows, cols = it_ref.shape
    partner = chip * CORES + 1 - core
    f32, bf16 = jnp.float32, jnp.bfloat16
    greet(nr, nc)
    sends = []
    order = [*range(1, chips), 0]
    for d in order:
        k = (chip + d) % chips
        send_a[d] = terms_ref[k * CORES + 1 - core].astype(bf16)
        copy = remote(send_a.at[d], recv_a.at[d], sa.at[d], ra.at[d], pc=partner)
        copy.start()
        sends.append(copy)
    for d in order:
        k = (chip + d) % chips
        remote(send_a.at[d], recv_a.at[d], sa.at[d], ra.at[d], pc=partner).wait_recv()
        summed = terms_ref[k * CORES + core] + recv_a[d].astype(f32)
        if d:
            send_b[d] = summed.astype(bf16)
            copy = remote(send_b.at[d], recv_b.at[d], sb.at[d], rb.at[d], pc=k * CORES + core)
            copy.start()
            sends.append(copy)
        else:
            kept[...] = summed
    for d in range(1, chips):
        peer = ((chip + d) % chips) * CORES + core
        remote(send_b.at[d], recv_b.at[d], sb.at[d], rb.at[d], pc=peer).wait_recv()
        kept[...] += recv_b[d].astype(f32)
    for d in range(1, nr):
        i = (r + d) % nr
        send_c[d] = kept[pl.ds(pl.multiple_of(i * rows, rows), rows)].astype(bf16)
        copy = remote(send_c.at[d], recv_c.at[d], sc.at[d], rc.at[d], pr=i)
        copy.start()
        sends.append(copy)
    own[...] = kept[pl.ds(pl.multiple_of(r * rows, rows), rows)]
    for d in range(1, nr):
        remote(send_c.at[d], recv_c.at[d], sc.at[d], rc.at[d], pr=(r + d) % nr).wait_recv()
        own[...] += recv_c[d].astype(f32)
    current = it_ref[...].astype(f32)
    residual = side_ref[...] - gap_ref[...] * current - own[...]
    out_ref[...] = (
        current
        + relax_weight * residual / gap_ref[...]
        + momentum * (current - prev_ref[...].astype(f32))
    )
    for copy in sends:
        copy.wait_send()


def reduce_update(nr, nc, terms, iterate, previous, right_side, energy_gap):
    rows, cols = iterate.shape
    no, chips = terms.shape[1], nc // CORES
    dma, bf16, f32 = pltpu.SemaphoreType.DMA, jnp.bfloat16, jnp.float32
    return pl.pallas_call(
        functools.partial(reduce_kernel, nr, nc),
        out_shape=jax.ShapeDtypeStruct((rows, cols), f32),
        in_specs=[pl.BlockSpec(memory_space=pltpu.VMEM)] * 5,
        out_specs=pl.BlockSpec(memory_space=pltpu.VMEM),
        scratch_shapes=[
            *[pltpu.VMEM((chips, no, cols), bf16)] * 4,
            *[pltpu.VMEM((nr, rows, cols), bf16)] * 2,
            pltpu.VMEM((no, cols), f32),
            pltpu.VMEM((rows, cols), f32),
            *[dma((chips,))] * 4,
            *[dma((nr,))] * 2,
        ],
        compiler_params=pltpu.CompilerParams(collective_id=1, has_side_effects=True),
        name="reduce",
    )(terms, iterate, previous, right_side, energy_gap)


def across(q, d, chips):
    out, bit = 0, 1
    while bit < chips:
        out = out + bit * ((q // bit + d // bit) % 2)
        bit *= 2
    return out


def visits(chips):
    return sorted(range(1, chips), key=lambda d: -bin(d).count("1"))


def fused_kernel(
    nr, nc, tm, tn, it_ref, occ_hbm, virt_hbm, screen_hbm, out_ref,
    occ, occ_t, virt, half, acc, tiles, full, parts, core_out, core_in, plane_out, plane_in, line_out, line_in, kept,
    load, tile_sem, own_sem, zs, zr, cs, cr, ps, pr_, sa, ra, sb, rb, sc, rc,
):
    r, c, chip, core, chips = place(nr, nc)
    rows, cols = it_ref.shape
    no = nr * rows
    wide = CORES * cols
    steps_m, steps_n = occ_hbm.shape[1] // tm, virt_hbm.shape[1] // tn
    f32, bf16 = jnp.float32, jnp.bfloat16
    partner = chip * CORES + 1 - core
    order = visits(chips)
    sub = min(512, tm)

    def chip_at(d):
        return across(chip, d, chips)

    def tile_copy(s):
        n, m = s // steps_m, s % steps_m
        source = screen_hbm.at[
            pl.ds(pl.multiple_of(m * tm, tm), tm), pl.ds(pl.multiple_of(n * tn, tn), tn)
        ]
        return pltpu.make_async_copy(source, tiles.at[s % 2], tile_sem.at[s % 2])

    def block(i, q, k):
        return full.at[
            q, pl.ds(pl.multiple_of(i * rows, rows), rows), pl.ds(pl.multiple_of(k * cols, cols), cols)
        ]

    occ_load = pltpu.make_async_copy(occ_hbm, occ, load.at[0])
    virt_load = pltpu.make_async_copy(virt_hbm, virt, load.at[1])
    occ_load.start()
    virt_load.start()
    tile_copy(0).start()
    greet(nr, nc)

    own = pltpu.make_async_copy(it_ref, block(r, chip, core), own_sem)
    own.start()
    sends = []

    def start(copy):
        copy.start()
        sends.append(copy)

    for d in range(1, nr):
        start(remote(it_ref, block(r, chip, core), zs.at[d], zr.at[d], pr=(r + d) % nr))

    def spread(e, source, i):
        for d in order:
            start(remote(
                source, block(i, chip, core), cs.at[d, e], cr.at[d, e], pc=chip_at(d) * CORES + core
            ))
        start(remote(source, block(i, chip, core), ps.at[0, e], pr_.at[0, e], pc=partner))

    spread(0, it_ref, r)

    for e in range(1, nr):
        i = (r - e + nr) % nr
        here = block(i, chip, core)
        remote(it_ref, here, zs.at[e], zr.at[e], pr=(r + e) % nr).wait_recv()
        spread(e, here, i)
    own.wait()

    occ_load.wait()
    turn = min(512, tm)

    @pl.loop(0, occ_hbm.shape[1] // turn)
    def _(j):
        at = pl.ds(pl.multiple_of(j * turn, turn), turn)
        occ_t[at] = occ[:, at].T

    def forward(d, e):
        q = chip_at(d)
        here = block((r - e + nr) % nr, q, core)
        remote(here, here, cs.at[d, e], cr.at[d, e], pc=q * CORES + core).wait_recv()
        start(remote(here, here, ps.at[d, e], pr_.at[d, e], pc=partner))

    def project(d):
        q = chip_at(d)
        for e in range(nr):
            there = block((r - e + nr) % nr, q, 1 - core)
            remote(there, there, ps.at[d, e], pr_.at[d, e], pc=partner).wait_recv()
        at_q = pl.ds(pl.multiple_of(q * wide, wide), wide)
        for j in range(0, virt_hbm.shape[1], tn):
            at = pl.ds(j, tn)
            term = jnp.dot(full[q], virt[at_q, at], preferred_element_type=f32)
            if d == 0:
                acc[:, at] = term
            elif d == order[-1]:
                half[:, at] = (acc[:, at] + term).astype(bf16)
            else:
                acc[:, at] += term

    virt_load.wait()
    project(0)
    for e in range(nr):
        for d in order:
            forward(d, e)
    for d in order:
        project(d)

    @pl.loop(0, steps_n * steps_m)
    def _(s):
        n, m = s // steps_m, s % steps_m
        tile_copy(s).wait()

        @pl.when(s + 1 < steps_n * steps_m)
        def _():
            tile_copy(s + 1).start()

        at_n = pl.ds(pl.multiple_of(n * tn, tn), tn)
        at_m = pl.ds(pl.multiple_of(m * tm, tm), tm)
        tile = tiles.at[s % 2]
        for j in range(0, tm, sub):
            turned = occ_t[pl.ds(pl.multiple_of(m * tm + j, sub), sub)]
            pair = jnp.dot(turned, half[:, at_n], preferred_element_type=f32)
            tile[j : j + sub] = (tile[j : j + sub].astype(f32) * pair).astype(bf16)
        back = jnp.dot(occ[:, at_m], tile[...], preferred_element_type=f32)
        acc[:, at_n] = jnp.where(m == 0, 0.0, acc[:, at_n]) + back

        @pl.when(m == steps_m - 1)
        def _():
            half[:, at_n] = acc[:, at_n].astype(bf16)

    bands = 2 if nr % 2 == 0 else 1
    tall = no // bands

    def band(ref, d, h):
        return ref.at[d, pl.ds(h * tall, tall)]

    def to_partner(d, h):
        return remote(band(core_out, d, h), band(core_in, d, h), sa.at[d, h], ra.at[d, h], pc=partner)

    def to_chip(d, h):
        return remote(
            band(plane_out, d, h), band(plane_in, d, h), sb.at[d, h], rb.at[d, h],
            pc=chip_at(d) * CORES + core,
        )

    def along(d):
        return remote(line_out.at[d], line_in.at[d], sc.at[d], rc.at[d], pr=(r + d) % nr)

    def fold(h, d):
        at = pl.ds(h * tall, tall)
        to_partner(d, h).wait_recv()
        summed = parts[d, core, at] + core_in[d, at].astype(f32)
        if d:
            plane_out[d, at] = summed.astype(bf16)
            start(to_chip(d, h))
        else:
            kept[at] = summed

    def product(h, d):
        q = chip_at(d)
        return lax.dot_general(
            half[h * tall : (h + 1) * tall], virt[pl.ds(pl.multiple_of(q * wide, wide), wide), :],
            (((1,), (1,)), ((), ())), preferred_element_type=f32,
        )

    ranks = [*order, 0]
    pieces = [(h, ranks[g : g + 2]) for h in range(bands) for g in range(0, chips, 2)]

    def fold_piece(h, group):
        for d in group:
            fold(h, d)

    for p, (h, group) in enumerate(pieces):
        at = pl.ds(h * tall, tall)
        terms = [product(h, d) for d in group]
        for d, term in zip(group, terms):
            for k in range(CORES):
                parts[d, k, at] = term[:, k * cols : (k + 1) * cols]
            core_out[d, at] = parts[d, 1 - core, at].astype(bf16)
        for d in group:
            start(to_partner(d, h))
        if p >= 1:
            fold_piece(*pieces[p - 1])
    for piece in pieces[-1:]:
        fold_piece(*piece)
    for h in range(bands):
        at = pl.ds(h * tall, tall)
        for d in order:
            to_chip(d, h).wait_recv()
            kept[at] += plane_in[d, at].astype(f32)
        for d in range(1, nr):
            i = (r + d) % nr

            @pl.when(i // (nr // bands) == h)
            def _():
                line_out[d] = kept[pl.ds(pl.multiple_of(i * rows, rows), rows)].astype(bf16)
                along(d).start()

    total = kept[pl.ds(pl.multiple_of(r * rows, rows), rows)]
    for d in range(1, nr):
        along(d).wait_recv()
        total = total + line_in[d].astype(f32)
    out_ref[...] = total
    for d in range(1, nr):
        along(d).wait_send()
    for copy in sends:
        copy.wait_send()


def fused(nr, nc, iterate, occ, virt, screening):
    rows, cols = iterate.shape
    no, nv, chips = nr * rows, nc * cols, nc // CORES
    tall, long = screening.shape
    tm, tn = min(2048, tall), min(1024, long)
    dma, bf16, f32 = pltpu.SemaphoreType.DMA, jnp.bfloat16, jnp.float32
    vmem = pltpu.VMEM
    return pl.pallas_call(
        functools.partial(fused_kernel, nr, nc, tm, tn),
        out_shape=jax.ShapeDtypeStruct((rows, cols), f32),
        in_specs=[pl.BlockSpec(memory_space=pltpu.VMEM)] + [pl.BlockSpec(memory_space=pl.ANY)] * 3,
        out_specs=pl.BlockSpec(memory_space=pltpu.VMEM),
        scratch_shapes=[
            vmem((no, tall), bf16),
            vmem((tall, no), bf16),
            vmem((nv, long), bf16),
            vmem((no, long), bf16),
            vmem((no, long), f32),
            vmem((2, tm, tn), bf16),
            vmem((chips, no, CORES * cols), bf16),
            vmem((chips, CORES, no, cols), f32),
            *[vmem((chips, no, cols), bf16)] * 4,
            *[vmem((nr, rows, cols), bf16)] * 2,
            vmem((no, cols), f32),
            dma((2,)),
            dma((2,)),
            dma,
            *[dma((nr,))] * 2,
            *[dma((chips, nr))] * 4,
            *[dma((chips, 2))] * 4,
            *[dma((nr,))] * 2,
        ],
        compiler_params=pltpu.CompilerParams(
            collective_id=0, has_side_effects=True, vmem_limit_bytes=63 << 20
        ),
        name="fused",
    )(iterate, occ, virt, screening)


def fits(nr, nc, iterate, screening):
    rows, cols = iterate.shape
    chips = nc // CORES
    return nc % CORES == 0 and chips > 1 and chips & (chips - 1) == 0 and rows % 16 == 0 and cols % 128 == 0


def solution(mesh):
    nr, nc = mesh.shape["pr"], mesh.shape["pc"]

    def on_device(iterate, previous, right_side, energy_gap, occ_points, virt_points, screening):
        if fits(nr, nc, iterate, screening):
            kernel = fused(nr, nc, iterate, occ_points, virt_points, screening)
            current = iterate.astype(jnp.float32)
            residual = right_side - energy_gap * current - kernel
            return (
                current
                + relax_weight * residual / energy_gap
                + momentum * (current - previous.astype(jnp.float32))
            )
        full = gather(nr, nc, iterate)
        terms = field(nc, full, occ_points, virt_points, screening)
        return reduce_update(nr, nc, terms, iterate, previous, right_side, energy_gap)

    return jax.shard_map(
        on_device,
        mesh=mesh,
        in_specs=(
            P("pr", "pc"),
            P("pr", "pc"),
            P("pr", "pc"),
            P("pr", "pc"),
            P(None, "pr"),
            P(None, "pc"),
            P("pr", "pc"),
        ),
        out_specs=P("pr", "pc"),
        check_vma=False,
    )
```

```python
import functools

import jax
import jax.numpy as jnp
from jax import lax
from jax.experimental import pallas as pl
from jax.experimental.pallas import tpu as pltpu
from jax.sharding import PartitionSpec as P

relax_weight = 0.8
momentum = 0.3
MESH = pl.DeviceIdType.MESH
CORES = 2


def place(nr, nc):
    r, c = lax.axis_index("pr"), lax.axis_index("pc")
    chips = nc // CORES
    return r, c, c // CORES, c % CORES, chips


def greet(nr, nc):
    r, c, chip, core, chips = place(nr, nc)
    barrier = pltpu.get_barrier_semaphore()
    for d in range(1, nr):
        pl.semaphore_signal(barrier, inc=1, device_id={"pr": (r + d) % nr}, device_id_type=MESH)
    for d in range(1, chips):
        peer = ((chip + d) % chips) * CORES + core
        pl.semaphore_signal(barrier, inc=1, device_id={"pc": peer}, device_id_type=MESH)
    pl.semaphore_signal(barrier, inc=1, device_id={"pc": chip * CORES + 1 - core}, device_id_type=MESH)
    pl.semaphore_wait(barrier, nr - 1 + chips)


def remote(src, dst, send, recv, **where):
    return pltpu.make_async_remote_copy(
        src_ref=src, dst_ref=dst, send_sem=send, recv_sem=recv, device_id=where, device_id_type=MESH
    )


def gather_kernel(nr, nc, flat, x_ref, out_ref, own_sem, zs, zr, cs, cr, ps, pr_):
    r, c, chip, core, chips = place(nr, nc)
    rows, cols = x_ref.shape
    partner = chip * CORES + 1 - core

    def column(j):
        if flat:
            return out_ref.at[:, pl.ds(pl.multiple_of(j * cols, cols), cols)]
        return out_ref.at[j]

    def block(i, j):
        own = pl.ds(pl.multiple_of(i * rows, rows), rows)
        if flat:
            return out_ref.at[own, pl.ds(pl.multiple_of(j * cols, cols), cols)]
        return out_ref.at[j, own]

    greet(nr, nc)
    keep = pltpu.make_async_copy(x_ref, block(r, c), own_sem)
    keep.start()
    along = [
        remote(x_ref, block(r, c), zs.at[d - 1], zr.at[d - 1], pr=(r + d) % nr) for d in range(1, nr)
    ]
    for copy in along:
        copy.start()
    keep.wait()
    for d in range(1, nr):
        remote(x_ref, block((r - d + nr) % nr, c), zs.at[d - 1], zr.at[d - 1], pr=(r + d) % nr).wait_recv()
    across = [
        remote(column(c), column(c), cs.at[d - 1], cr.at[d - 1], pc=((chip + d) % chips) * CORES + core)
        for d in range(1, chips)
    ]
    for copy in across:
        copy.start()
    over = [remote(column(c), column(c), ps.at[0], pr_.at[0], pc=partner)]
    over[0].start()
    for d in range(1, chips):
        j = ((chip - d + chips) % chips) * CORES + core
        remote(column(j), column(j), cs.at[d - 1], cr.at[d - 1], pc=partner).wait_recv()
        copy = remote(column(j), column(j), ps.at[d], pr_.at[d], pc=partner)
        copy.start()
        over.append(copy)
    for d in range(chips):
        j = ((chip - d + chips) % chips) * CORES + 1 - core
        remote(column(j), column(j), ps.at[d], pr_.at[d], pc=partner).wait_recv()
    for copy in along + across + over:
        copy.wait_send()


def gather(nr, nc, x):
    rows, cols = x.shape
    chips = nc // CORES
    flat = cols % 128 == 0
    shape = (nr * rows, nc * cols) if flat else (nc, nr * rows, cols)
    dma = pltpu.SemaphoreType.DMA
    full = pl.pallas_call(
        functools.partial(gather_kernel, nr, nc, flat),
        out_shape=jax.ShapeDtypeStruct(shape, x.dtype),
        in_specs=[pl.BlockSpec(memory_space=pltpu.VMEM)],
        out_specs=pl.BlockSpec(memory_space=pltpu.VMEM),
        scratch_shapes=[
            dma, dma((nr,)), dma((nr,)), dma((chips,)), dma((chips,)), dma((chips,)), dma((chips,)),
        ],
        compiler_params=pltpu.CompilerParams(collective_id=0, has_side_effects=True),
        name="gather",
    )(x)
    return full if flat else full.transpose(1, 0, 2).reshape(nr * rows, nc * cols)


def field_kernel(it_ref, virt_ref, occ_ref, screen_ref, out_ref, occ_t, half, back, total):
    n, m = pl.program_id(0), pl.program_id(1)
    last_n, last_m = pl.num_programs(0) - 1, pl.num_programs(1) - 1
    f32, bf16 = jnp.float32, jnp.bfloat16

    @pl.when(m == 0)
    def _():
        half[...] = jnp.dot(it_ref[...], virt_ref[...], preferred_element_type=f32).astype(bf16)
        back[...] = jnp.zeros_like(back)

    @pl.when((m == 0) & (n == 0))
    def _():
        total[...] = jnp.zeros_like(total)

    def work(turned):
        pair = jnp.dot(turned, half[...], preferred_element_type=f32)
        screened = (screen_ref[...].astype(f32) * pair).astype(bf16)
        back[...] += jnp.dot(occ_ref[...], screened, preferred_element_type=f32)

    @pl.when(n == 0)
    def _():
        turned = occ_ref[...].T
        occ_t[m] = turned
        work(turned)

    @pl.when(n != 0)
    def _():
        work(occ_t[m])

    @pl.when(m == last_m)
    def _():
        total[...] += lax.dot_general(
            back[...].astype(bf16), virt_ref[...], (((1,), (1,)), ((), ())), preferred_element_type=f32
        )

    @pl.when((m == last_m) & (n == last_n))
    def _():
        if len(out_ref.shape) == 3:
            parts, _, cols = out_ref.shape
            for q in range(parts):
                out_ref[q] = total[:, q * cols : (q + 1) * cols]
        else:
            out_ref[...] = total[...]


def field(nc, full, occ, virt, screening):
    no, nv = full.shape
    rows, cols = screening.shape
    tm, tn = min(2048, rows), min(1024, cols)
    wide = nv // nc
    shape = (nc, no, wide) if wide % 128 == 0 else (no, nv)
    out = pl.pallas_call(
        field_kernel,
        out_shape=jax.ShapeDtypeStruct(shape, jnp.float32),
        grid=(cols // tn, rows // tm),
        in_specs=[
            pl.BlockSpec((no, nv), lambda n, m: (0, 0)),
            pl.BlockSpec((nv, tn), lambda n, m: (0, n)),
            pl.BlockSpec((no, tm), lambda n, m: (0, m)),
            pl.BlockSpec((tm, tn), lambda n, m: (m, n)),
        ],
        out_specs=pl.BlockSpec(shape, lambda n, m: (0,) * len(shape)),
        scratch_shapes=[
            pltpu.VMEM((rows // tm, tm, no), jnp.bfloat16),
            pltpu.VMEM((no, tn), jnp.bfloat16),
            pltpu.VMEM((no, tn), jnp.float32),
            pltpu.VMEM((no, nv), jnp.float32),
        ],
        compiler_params=pltpu.CompilerParams(
            dimension_semantics=("arbitrary", "arbitrary"), vmem_limit_bytes=63 << 20
        ),
        name="field",
    )(full, virt, occ, screening)
    return out if wide % 128 == 0 else out.reshape(no, nc, wide).transpose(1, 0, 2)


def reduce_kernel(
    nr, nc, terms_ref, it_ref, prev_ref, side_ref, gap_ref, out_ref,
    send_a, recv_a, send_b, recv_b, send_c, recv_c, kept, own, sa, ra, sb, rb, sc, rc,
):
    r, c, chip, core, chips = place(nr, nc)
    rows, cols = it_ref.shape
    partner = chip * CORES + 1 - core
    f32, bf16 = jnp.float32, jnp.bfloat16
    greet(nr, nc)
    sends = []
    order = [*range(1, chips), 0]
    for d in order:
        k = (chip + d) % chips
        send_a[d] = terms_ref[k * CORES + 1 - core].astype(bf16)
        copy = remote(send_a.at[d], recv_a.at[d], sa.at[d], ra.at[d], pc=partner)
        copy.start()
        sends.append(copy)
    for d in order:
        k = (chip + d) % chips
        remote(send_a.at[d], recv_a.at[d], sa.at[d], ra.at[d], pc=partner).wait_recv()
        summed = terms_ref[k * CORES + core] + recv_a[d].astype(f32)
        if d:
            send_b[d] = summed.astype(bf16)
            copy = remote(send_b.at[d], recv_b.at[d], sb.at[d], rb.at[d], pc=k * CORES + core)
            copy.start()
            sends.append(copy)
        else:
            kept[...] = summed
    for d in range(1, chips):
        peer = ((chip + d) % chips) * CORES + core
        remote(send_b.at[d], recv_b.at[d], sb.at[d], rb.at[d], pc=peer).wait_recv()
        kept[...] += recv_b[d].astype(f32)
    for d in range(1, nr):
        i = (r + d) % nr
        send_c[d] = kept[pl.ds(pl.multiple_of(i * rows, rows), rows)].astype(bf16)
        copy = remote(send_c.at[d], recv_c.at[d], sc.at[d], rc.at[d], pr=i)
        copy.start()
        sends.append(copy)
    own[...] = kept[pl.ds(pl.multiple_of(r * rows, rows), rows)]
    for d in range(1, nr):
        remote(send_c.at[d], recv_c.at[d], sc.at[d], rc.at[d], pr=(r + d) % nr).wait_recv()
        own[...] += recv_c[d].astype(f32)
    current = it_ref[...].astype(f32)
    residual = side_ref[...] - gap_ref[...] * current - own[...]
    out_ref[...] = (
        current
        + relax_weight * residual / gap_ref[...]
        + momentum * (current - prev_ref[...].astype(f32))
    )
    for copy in sends:
        copy.wait_send()


def reduce_update(nr, nc, terms, iterate, previous, right_side, energy_gap):
    rows, cols = iterate.shape
    no, chips = terms.shape[1], nc // CORES
    dma, bf16, f32 = pltpu.SemaphoreType.DMA, jnp.bfloat16, jnp.float32
    return pl.pallas_call(
        functools.partial(reduce_kernel, nr, nc),
        out_shape=jax.ShapeDtypeStruct((rows, cols), f32),
        in_specs=[pl.BlockSpec(memory_space=pltpu.VMEM)] * 5,
        out_specs=pl.BlockSpec(memory_space=pltpu.VMEM),
        scratch_shapes=[
            *[pltpu.VMEM((chips, no, cols), bf16)] * 4,
            *[pltpu.VMEM((nr, rows, cols), bf16)] * 2,
            pltpu.VMEM((no, cols), f32),
            pltpu.VMEM((rows, cols), f32),
            *[dma((chips,))] * 4,
            *[dma((nr,))] * 2,
        ],
        compiler_params=pltpu.CompilerParams(collective_id=1, has_side_effects=True),
        name="reduce",
    )(terms, iterate, previous, right_side, energy_gap)


def across(q, d, chips):
    out, bit = 0, 1
    while bit < chips:
        out = out + bit * ((q // bit + d // bit) % 2)
        bit *= 2
    return out


def visits(chips):
    return sorted(range(1, chips), key=lambda d: -bin(d).count("1"))


def fused_kernel(
    nr, nc, tm, tn, it_ref, occ_hbm, virt_hbm, screen_hbm, out_ref,
    occ, occ_t, virt, half, rear, acc, tiles, full, parts, core_out, core_in, plane_out, plane_in, line_out, line_in, kept,
    load, tile_sem, own_sem, zs, zr, cs, cr, ps, pr_, sa, ra, sb, rb, sc, rc,
):
    r, c, chip, core, chips = place(nr, nc)
    rows, cols = it_ref.shape
    no = nr * rows
    wide = CORES * cols
    steps_m, steps_n = occ_hbm.shape[1] // tm, virt_hbm.shape[1] // tn
    f32, bf16 = jnp.float32, jnp.bfloat16
    partner = chip * CORES + 1 - core
    order = visits(chips)
    sub = min(512, tm)

    def chip_at(d):
        return across(chip, d, chips)

    def tile_copy(s):
        n, m = s // steps_m, s % steps_m
        source = screen_hbm.at[
            pl.ds(pl.multiple_of(m * tm, tm), tm), pl.ds(pl.multiple_of(n * tn, tn), tn)
        ]
        return pltpu.make_async_copy(source, tiles.at[s % 2], tile_sem.at[s % 2])

    def block(i, q, k):
        return full.at[
            q, pl.ds(pl.multiple_of(i * rows, rows), rows), pl.ds(pl.multiple_of(k * cols, cols), cols)
        ]

    occ_load = pltpu.make_async_copy(occ_hbm, occ, load.at[0])
    virt_load = pltpu.make_async_copy(virt_hbm, virt, load.at[1])
    occ_load.start()
    virt_load.start()
    tile_copy(0).start()
    greet(nr, nc)

    own = pltpu.make_async_copy(it_ref, block(r, chip, core), own_sem)
    own.start()
    sends = []

    def start(copy):
        copy.start()
        sends.append(copy)

    for d in range(1, nr):
        start(remote(it_ref, block(r, chip, core), zs.at[d], zr.at[d], pr=(r + d) % nr))

    def spread(e, source, i):
        for d in order:
            start(remote(
                source, block(i, chip, core), cs.at[d, e], cr.at[d, e], pc=chip_at(d) * CORES + core
            ))
        start(remote(source, block(i, chip, core), ps.at[0, e], pr_.at[0, e], pc=partner))

    spread(0, it_ref, r)

    for e in range(1, nr):
        i = (r - e + nr) % nr
        here = block(i, chip, core)
        remote(it_ref, here, zs.at[e], zr.at[e], pr=(r + e) % nr).wait_recv()
        spread(e, here, i)
    own.wait()

    occ_load.wait()
    turn = min(512, tm)

    @pl.loop(0, occ_hbm.shape[1] // turn)
    def _(j):
        at = pl.ds(pl.multiple_of(j * turn, turn), turn)
        occ_t[at] = occ[:, at].T

    def forward(d, e):
        q = chip_at(d)
        here = block((r - e + nr) % nr, q, core)
        remote(here, here, cs.at[d, e], cr.at[d, e], pc=q * CORES + core).wait_recv()
        start(remote(here, here, ps.at[d, e], pr_.at[d, e], pc=partner))

    def project(d):
        q = chip_at(d)
        for e in range(nr):
            there = block((r - e + nr) % nr, q, 1 - core)
            remote(there, there, ps.at[d, e], pr_.at[d, e], pc=partner).wait_recv()
        at_q = pl.ds(pl.multiple_of(q * wide, wide), wide)
        for j in range(0, virt_hbm.shape[1], tn):
            at = pl.ds(j, tn)
            term = jnp.dot(full[q], virt[at_q, at], preferred_element_type=f32)
            if d == 0:
                acc[:, at] = term
            elif d == order[-1]:
                half[:, at] = (acc[:, at] + term).astype(bf16)
            else:
                acc[:, at] += term

    virt_load.wait()
    project(0)
    for e in range(nr):
        for d in order:
            forward(d, e)
    for d in order:
        project(d)

    last = steps_n * steps_m - 1

    def screen(s):
        n, m = s // steps_m, s % steps_m
        at_n = pl.ds(pl.multiple_of(n * tn, tn), tn)
        tile = tiles.at[s % 2]
        for j in range(0, tm, sub):
            turned = occ_t[pl.ds(pl.multiple_of(m * tm + j, sub), sub)]
            pair = jnp.dot(turned, half[:, at_n], preferred_element_type=f32)
            tile[j : j + sub] = (tile[j : j + sub].astype(f32) * pair).astype(bf16)

    def collect(s, at_i, keep):
        n, m = s // steps_m, s % steps_m
        at_n = pl.ds(pl.multiple_of(n * tn, tn), tn)
        at_m = pl.ds(pl.multiple_of(m * tm, tm), tm)
        back = jnp.dot(occ[at_i, at_m], tiles[s % 2], preferred_element_type=f32)
        summed = jnp.where(m == 0, 0.0, acc[at_i, at_n]) + back
        if keep:
            acc[at_i, at_n] = summed
        rear[at_i, at_n] = summed.astype(bf16)

    @pl.loop(0, last)
    def _(s):
        tile_copy(s).wait()
        tile_copy(s + 1).start()
        screen(s)
        collect(s, pl.ds(0, no), True)

    tile_copy(last).wait()
    screen(last)
    bands = 2 if nr % 2 == 0 else 1
    tall = no // bands

    def band(ref, d, h):
        return ref.at[d, pl.ds(h * tall, tall)]

    def to_partner(d, h):
        return remote(band(core_out, d, h), band(core_in, d, h), sa.at[d, h], ra.at[d, h], pc=partner)

    def to_chip(d, h):
        return remote(
            band(plane_out, d, h), band(plane_in, d, h), sb.at[d, h], rb.at[d, h],
            pc=chip_at(d) * CORES + core,
        )

    def along(d):
        return remote(line_out.at[d], line_in.at[d], sc.at[d], rc.at[d], pr=(r + d) % nr)

    def fold(h, d):
        at = pl.ds(h * tall, tall)
        to_partner(d, h).wait_recv()
        summed = parts[d, core, at] + core_in[d, at].astype(f32)
        if d:
            plane_out[d, at] = summed.astype(bf16)
            start(to_chip(d, h))
        else:
            kept[at] = summed

    def product(h, d):
        q = chip_at(d)
        return lax.dot_general(
            rear[h * tall : (h + 1) * tall], virt[pl.ds(pl.multiple_of(q * wide, wide), wide), :],
            (((1,), (1,)), ((), ())), preferred_element_type=f32,
        )

    ranks = [*order, 0]
    pieces = [(h, ranks[g : g + 2]) for h in range(bands) for g in range(0, chips, 2)]

    def fold_piece(h, group):
        for d in group:
            fold(h, d)

    for p, (h, group) in enumerate(pieces):
        at = pl.ds(h * tall, tall)
        if group[0] == ranks[0]:
            collect(last, at, False)
        terms = [product(h, d) for d in group]
        for d, term in zip(group, terms):
            for k in range(CORES):
                parts[d, k, at] = term[:, k * cols : (k + 1) * cols]
            core_out[d, at] = parts[d, 1 - core, at].astype(bf16)
        for d in group:
            start(to_partner(d, h))
        if p >= 1:
            fold_piece(*pieces[p - 1])
    for piece in pieces[-1:]:
        fold_piece(*piece)
    for h in range(bands):
        at = pl.ds(h * tall, tall)
        for d in order:
            to_chip(d, h).wait_recv()
            kept[at] += plane_in[d, at].astype(f32)
        for d in range(1, nr):
            i = (r + d) % nr

            @pl.when(i // (nr // bands) == h)
            def _():
                line_out[d] = kept[pl.ds(pl.multiple_of(i * rows, rows), rows)].astype(bf16)
                along(d).start()

    total = kept[pl.ds(pl.multiple_of(r * rows, rows), rows)]
    for d in range(1, nr):
        along(d).wait_recv()
        total = total + line_in[d].astype(f32)
    out_ref[...] = total
    for d in range(1, nr):
        along(d).wait_send()
    for copy in sends:
        copy.wait_send()


def fused(nr, nc, iterate, occ, virt, screening):
    rows, cols = iterate.shape
    no, nv, chips = nr * rows, nc * cols, nc // CORES
    tall, long = screening.shape
    tm, tn = min(2048, tall), min(1024, long)
    dma, bf16, f32 = pltpu.SemaphoreType.DMA, jnp.bfloat16, jnp.float32
    vmem = pltpu.VMEM
    return pl.pallas_call(
        functools.partial(fused_kernel, nr, nc, tm, tn),
        out_shape=jax.ShapeDtypeStruct((rows, cols), f32),
        in_specs=[pl.BlockSpec(memory_space=pltpu.VMEM)] + [pl.BlockSpec(memory_space=pl.ANY)] * 3,
        out_specs=pl.BlockSpec(memory_space=pltpu.VMEM),
        scratch_shapes=[
            vmem((no, tall), bf16),
            vmem((tall, no), bf16),
            vmem((nv, long), bf16),
            *[vmem((no, long), bf16)] * 2,
            vmem((no, long), f32),
            vmem((2, tm, tn), bf16),
            vmem((chips, no, CORES * cols), bf16),
            vmem((chips, CORES, no, cols), f32),
            *[vmem((chips, no, cols), bf16)] * 4,
            *[vmem((nr, rows, cols), bf16)] * 2,
            vmem((no, cols), f32),
            dma((2,)),
            dma((2,)),
            dma,
            *[dma((nr,))] * 2,
            *[dma((chips, nr))] * 4,
            *[dma((chips, 2))] * 4,
            *[dma((nr,))] * 2,
        ],
        compiler_params=pltpu.CompilerParams(
            collective_id=0, has_side_effects=True, vmem_limit_bytes=63 << 20
        ),
        name="fused",
    )(iterate, occ, virt, screening)


def fits(nr, nc, iterate, screening):
    rows, cols = iterate.shape
    chips = nc // CORES
    return nc % CORES == 0 and chips > 1 and chips & (chips - 1) == 0 and rows % 16 == 0 and cols % 128 == 0


def solution(mesh):
    nr, nc = mesh.shape["pr"], mesh.shape["pc"]

    def on_device(iterate, previous, right_side, energy_gap, occ_points, virt_points, screening):
        if fits(nr, nc, iterate, screening):
            kernel = fused(nr, nc, iterate, occ_points, virt_points, screening)
            current = iterate.astype(jnp.float32)
            residual = right_side - energy_gap * current - kernel
            return (
                current
                + relax_weight * residual / energy_gap
                + momentum * (current - previous.astype(jnp.float32))
            )
        full = gather(nr, nc, iterate)
        terms = field(nc, full, occ_points, virt_points, screening)
        return reduce_update(nr, nc, terms, iterate, previous, right_side, energy_gap)

    return jax.shard_map(
        on_device,
        mesh=mesh,
        in_specs=(
            P("pr", "pc"),
            P("pr", "pc"),
            P("pr", "pc"),
            P("pr", "pc"),
            P(None, "pr"),
            P(None, "pc"),
            P("pr", "pc"),
        ),
        out_specs=P("pr", "pc"),
        check_vma=False,
    )
```

```python
import functools

import jax
import jax.numpy as jnp
from jax import lax
from jax.experimental import pallas as pl
from jax.experimental.pallas import tpu as pltpu
from jax.sharding import PartitionSpec as P

relax_weight = 0.8
momentum = 0.3
MESH = pl.DeviceIdType.MESH
CORES = 2


def place(nr, nc):
    r, c = lax.axis_index("pr"), lax.axis_index("pc")
    chips = nc // CORES
    return r, c, c // CORES, c % CORES, chips


def greet(nr, nc):
    r, c, chip, core, chips = place(nr, nc)
    barrier = pltpu.get_barrier_semaphore()
    for d in range(1, nr):
        pl.semaphore_signal(barrier, inc=1, device_id={"pr": (r + d) % nr}, device_id_type=MESH)
    for d in range(1, chips):
        peer = ((chip + d) % chips) * CORES + core
        pl.semaphore_signal(barrier, inc=1, device_id={"pc": peer}, device_id_type=MESH)
    pl.semaphore_signal(barrier, inc=1, device_id={"pc": chip * CORES + 1 - core}, device_id_type=MESH)
    pl.semaphore_wait(barrier, nr - 1 + chips)


def remote(src, dst, send, recv, **where):
    return pltpu.make_async_remote_copy(
        src_ref=src, dst_ref=dst, send_sem=send, recv_sem=recv, device_id=where, device_id_type=MESH
    )


def gather_kernel(nr, nc, flat, x_ref, out_ref, own_sem, zs, zr, cs, cr, ps, pr_):
    r, c, chip, core, chips = place(nr, nc)
    rows, cols = x_ref.shape
    partner = chip * CORES + 1 - core

    def column(j):
        if flat:
            return out_ref.at[:, pl.ds(pl.multiple_of(j * cols, cols), cols)]
        return out_ref.at[j]

    def block(i, j):
        own = pl.ds(pl.multiple_of(i * rows, rows), rows)
        if flat:
            return out_ref.at[own, pl.ds(pl.multiple_of(j * cols, cols), cols)]
        return out_ref.at[j, own]

    greet(nr, nc)
    keep = pltpu.make_async_copy(x_ref, block(r, c), own_sem)
    keep.start()
    along = [
        remote(x_ref, block(r, c), zs.at[d - 1], zr.at[d - 1], pr=(r + d) % nr) for d in range(1, nr)
    ]
    for copy in along:
        copy.start()
    keep.wait()
    for d in range(1, nr):
        remote(x_ref, block((r - d + nr) % nr, c), zs.at[d - 1], zr.at[d - 1], pr=(r + d) % nr).wait_recv()
    across = [
        remote(column(c), column(c), cs.at[d - 1], cr.at[d - 1], pc=((chip + d) % chips) * CORES + core)
        for d in range(1, chips)
    ]
    for copy in across:
        copy.start()
    over = [remote(column(c), column(c), ps.at[0], pr_.at[0], pc=partner)]
    over[0].start()
    for d in range(1, chips):
        j = ((chip - d + chips) % chips) * CORES + core
        remote(column(j), column(j), cs.at[d - 1], cr.at[d - 1], pc=partner).wait_recv()
        copy = remote(column(j), column(j), ps.at[d], pr_.at[d], pc=partner)
        copy.start()
        over.append(copy)
    for d in range(chips):
        j = ((chip - d + chips) % chips) * CORES + 1 - core
        remote(column(j), column(j), ps.at[d], pr_.at[d], pc=partner).wait_recv()
    for copy in along + across + over:
        copy.wait_send()


def gather(nr, nc, x):
    rows, cols = x.shape
    chips = nc // CORES
    flat = cols % 128 == 0
    shape = (nr * rows, nc * cols) if flat else (nc, nr * rows, cols)
    dma = pltpu.SemaphoreType.DMA
    full = pl.pallas_call(
        functools.partial(gather_kernel, nr, nc, flat),
        out_shape=jax.ShapeDtypeStruct(shape, x.dtype),
        in_specs=[pl.BlockSpec(memory_space=pltpu.VMEM)],
        out_specs=pl.BlockSpec(memory_space=pltpu.VMEM),
        scratch_shapes=[
            dma, dma((nr,)), dma((nr,)), dma((chips,)), dma((chips,)), dma((chips,)), dma((chips,)),
        ],
        compiler_params=pltpu.CompilerParams(collective_id=0, has_side_effects=True),
        name="gather",
    )(x)
    return full if flat else full.transpose(1, 0, 2).reshape(nr * rows, nc * cols)


def field_kernel(it_ref, virt_ref, occ_ref, screen_ref, out_ref, occ_t, half, back, total):
    n, m = pl.program_id(0), pl.program_id(1)
    last_n, last_m = pl.num_programs(0) - 1, pl.num_programs(1) - 1
    f32, bf16 = jnp.float32, jnp.bfloat16

    @pl.when(m == 0)
    def _():
        half[...] = jnp.dot(it_ref[...], virt_ref[...], preferred_element_type=f32).astype(bf16)
        back[...] = jnp.zeros_like(back)

    @pl.when((m == 0) & (n == 0))
    def _():
        total[...] = jnp.zeros_like(total)

    def work(turned):
        pair = jnp.dot(turned, half[...], preferred_element_type=f32)
        screened = (screen_ref[...].astype(f32) * pair).astype(bf16)
        back[...] += jnp.dot(occ_ref[...], screened, preferred_element_type=f32)

    @pl.when(n == 0)
    def _():
        turned = occ_ref[...].T
        occ_t[m] = turned
        work(turned)

    @pl.when(n != 0)
    def _():
        work(occ_t[m])

    @pl.when(m == last_m)
    def _():
        total[...] += lax.dot_general(
            back[...].astype(bf16), virt_ref[...], (((1,), (1,)), ((), ())), preferred_element_type=f32
        )

    @pl.when((m == last_m) & (n == last_n))
    def _():
        if len(out_ref.shape) == 3:
            parts, _, cols = out_ref.shape
            for q in range(parts):
                out_ref[q] = total[:, q * cols : (q + 1) * cols]
        else:
            out_ref[...] = total[...]


def field(nc, full, occ, virt, screening):
    no, nv = full.shape
    rows, cols = screening.shape
    tm, tn = min(2048, rows), min(1024, cols)
    wide = nv // nc
    shape = (nc, no, wide) if wide % 128 == 0 else (no, nv)
    out = pl.pallas_call(
        field_kernel,
        out_shape=jax.ShapeDtypeStruct(shape, jnp.float32),
        grid=(cols // tn, rows // tm),
        in_specs=[
            pl.BlockSpec((no, nv), lambda n, m: (0, 0)),
            pl.BlockSpec((nv, tn), lambda n, m: (0, n)),
            pl.BlockSpec((no, tm), lambda n, m: (0, m)),
            pl.BlockSpec((tm, tn), lambda n, m: (m, n)),
        ],
        out_specs=pl.BlockSpec(shape, lambda n, m: (0,) * len(shape)),
        scratch_shapes=[
            pltpu.VMEM((rows // tm, tm, no), jnp.bfloat16),
            pltpu.VMEM((no, tn), jnp.bfloat16),
            pltpu.VMEM((no, tn), jnp.float32),
            pltpu.VMEM((no, nv), jnp.float32),
        ],
        compiler_params=pltpu.CompilerParams(
            dimension_semantics=("arbitrary", "arbitrary"), vmem_limit_bytes=63 << 20
        ),
        name="field",
    )(full, virt, occ, screening)
    return out if wide % 128 == 0 else out.reshape(no, nc, wide).transpose(1, 0, 2)


def reduce_kernel(
    nr, nc, terms_ref, it_ref, prev_ref, side_ref, gap_ref, out_ref,
    send_a, recv_a, send_b, recv_b, send_c, recv_c, kept, own, sa, ra, sb, rb, sc, rc,
):
    r, c, chip, core, chips = place(nr, nc)
    rows, cols = it_ref.shape
    partner = chip * CORES + 1 - core
    f32, bf16 = jnp.float32, jnp.bfloat16
    greet(nr, nc)
    sends = []
    order = [*range(1, chips), 0]
    for d in order:
        k = (chip + d) % chips
        send_a[d] = terms_ref[k * CORES + 1 - core].astype(bf16)
        copy = remote(send_a.at[d], recv_a.at[d], sa.at[d], ra.at[d], pc=partner)
        copy.start()
        sends.append(copy)
    for d in order:
        k = (chip + d) % chips
        remote(send_a.at[d], recv_a.at[d], sa.at[d], ra.at[d], pc=partner).wait_recv()
        summed = terms_ref[k * CORES + core] + recv_a[d].astype(f32)
        if d:
            send_b[d] = summed.astype(bf16)
            copy = remote(send_b.at[d], recv_b.at[d], sb.at[d], rb.at[d], pc=k * CORES + core)
            copy.start()
            sends.append(copy)
        else:
            kept[...] = summed
    for d in range(1, chips):
        peer = ((chip + d) % chips) * CORES + core
        remote(send_b.at[d], recv_b.at[d], sb.at[d], rb.at[d], pc=peer).wait_recv()
        kept[...] += recv_b[d].astype(f32)
    for d in range(1, nr):
        i = (r + d) % nr
        send_c[d] = kept[pl.ds(pl.multiple_of(i * rows, rows), rows)].astype(bf16)
        copy = remote(send_c.at[d], recv_c.at[d], sc.at[d], rc.at[d], pr=i)
        copy.start()
        sends.append(copy)
    own[...] = kept[pl.ds(pl.multiple_of(r * rows, rows), rows)]
    for d in range(1, nr):
        remote(send_c.at[d], recv_c.at[d], sc.at[d], rc.at[d], pr=(r + d) % nr).wait_recv()
        own[...] += recv_c[d].astype(f32)
    current = it_ref[...].astype(f32)
    residual = side_ref[...] - gap_ref[...] * current - own[...]
    out_ref[...] = (
        current
        + relax_weight * residual / gap_ref[...]
        + momentum * (current - prev_ref[...].astype(f32))
    )
    for copy in sends:
        copy.wait_send()


def reduce_update(nr, nc, terms, iterate, previous, right_side, energy_gap):
    rows, cols = iterate.shape
    no, chips = terms.shape[1], nc // CORES
    dma, bf16, f32 = pltpu.SemaphoreType.DMA, jnp.bfloat16, jnp.float32
    return pl.pallas_call(
        functools.partial(reduce_kernel, nr, nc),
        out_shape=jax.ShapeDtypeStruct((rows, cols), f32),
        in_specs=[pl.BlockSpec(memory_space=pltpu.VMEM)] * 5,
        out_specs=pl.BlockSpec(memory_space=pltpu.VMEM),
        scratch_shapes=[
            *[pltpu.VMEM((chips, no, cols), bf16)] * 4,
            *[pltpu.VMEM((nr, rows, cols), bf16)] * 2,
            pltpu.VMEM((no, cols), f32),
            pltpu.VMEM((rows, cols), f32),
            *[dma((chips,))] * 4,
            *[dma((nr,))] * 2,
        ],
        compiler_params=pltpu.CompilerParams(collective_id=1, has_side_effects=True),
        name="reduce",
    )(terms, iterate, previous, right_side, energy_gap)


def across(q, d, chips):
    out, bit = 0, 1
    while bit < chips:
        out = out + bit * ((q // bit + d // bit) % 2)
        bit *= 2
    return out


def visits(chips):
    return sorted(range(1, chips), key=lambda d: -bin(d).count("1"))


def fused_kernel(
    nr, nc, tm, tn, it_ref, occ_hbm, virt_hbm, screen_hbm, out_ref,
    occ, occ_t, virt, half, rear, acc, tiles, full, parts, core_out, core_in, plane_out, plane_in, line_out, line_in, kept,
    load, tile_sem, own_sem, zs, zr, cs, cr, ps, pr_, sa, ra, sb, rb, sc, rc,
):
    r, c, chip, core, chips = place(nr, nc)
    rows, cols = it_ref.shape
    no = nr * rows
    wide = CORES * cols
    steps_m, steps_n = occ_hbm.shape[1] // tm, virt_hbm.shape[1] // tn
    f32, bf16 = jnp.float32, jnp.bfloat16
    partner = chip * CORES + 1 - core
    order = visits(chips)
    sub = min(512, tm)

    def chip_at(d):
        return across(chip, d, chips)

    def tile_copy(s):
        n, m = s // steps_m, s % steps_m
        source = screen_hbm.at[
            pl.ds(pl.multiple_of(m * tm, tm), tm), pl.ds(pl.multiple_of(n * tn, tn), tn)
        ]
        return pltpu.make_async_copy(source, tiles.at[s % 2], tile_sem.at[s % 2])

    def block(i, q, k):
        return full.at[
            q, pl.ds(pl.multiple_of(i * rows, rows), rows), pl.ds(pl.multiple_of(k * cols, cols), cols)
        ]

    occ_load = pltpu.make_async_copy(occ_hbm, occ, load.at[0])
    virt_load = pltpu.make_async_copy(virt_hbm, virt, load.at[1])
    occ_load.start()
    virt_load.start()
    tile_copy(0).start()
    greet(nr, nc)

    own = pltpu.make_async_copy(it_ref, block(r, chip, core), own_sem)
    own.start()
    sends = []

    def start(copy):
        copy.start()
        sends.append(copy)

    for d in range(1, nr):
        start(remote(it_ref, block(r, chip, core), zs.at[d], zr.at[d], pr=(r + d) % nr))

    def spread(e, source, i):
        for d in order:
            start(remote(
                source, block(i, chip, core), cs.at[d, e], cr.at[d, e], pc=chip_at(d) * CORES + core
            ))
        start(remote(source, block(i, chip, core), ps.at[0, e], pr_.at[0, e], pc=partner))

    spread(0, it_ref, r)

    for e in range(1, nr):
        i = (r - e + nr) % nr
        here = block(i, chip, core)
        remote(it_ref, here, zs.at[e], zr.at[e], pr=(r + e) % nr).wait_recv()
        spread(e, here, i)
    own.wait()

    occ_load.wait()
    turn = min(512, tm)

    @pl.loop(0, occ_hbm.shape[1] // turn)
    def _(j):
        at = pl.ds(pl.multiple_of(j * turn, turn), turn)
        occ_t[at] = occ[:, at].T

    def forward(d, e):
        q = chip_at(d)
        here = block((r - e + nr) % nr, q, core)
        remote(here, here, cs.at[d, e], cr.at[d, e], pc=q * CORES + core).wait_recv()
        start(remote(here, here, ps.at[d, e], pr_.at[d, e], pc=partner))

    def project(group):
        for d in group:
            for e in range(nr):
                there = block((r - e + nr) % nr, chip_at(d), 1 - core)
                remote(there, there, ps.at[d, e], pr_.at[d, e], pc=partner).wait_recv()
        for j in range(0, virt_hbm.shape[1], tn):
            at = pl.ds(j, tn)
            term = sum(
                jnp.dot(
                    full[chip_at(d)],
                    virt[pl.ds(pl.multiple_of(chip_at(d) * wide, wide), wide), at],
                    preferred_element_type=f32,
                )
                for d in group
            )
            if group[0] == 0:
                acc[:, at] = term
            elif group[-1] == order[-1]:
                half[:, at] = (acc[:, at] + term).astype(bf16)
            else:
                acc[:, at] += term

    virt_load.wait()
    project([0])
    for e in range(nr):
        for d in order:
            forward(d, e)
    project(order)

    last = steps_n * steps_m - 1

    def screen(s):
        n, m = s // steps_m, s % steps_m
        at_n = pl.ds(pl.multiple_of(n * tn, tn), tn)
        tile = tiles.at[s % 2]
        for j in range(0, tm, sub):
            turned = occ_t[pl.ds(pl.multiple_of(m * tm + j, sub), sub)]
            pair = jnp.dot(turned, half[:, at_n], preferred_element_type=f32)
            tile[j : j + sub] = (tile[j : j + sub].astype(f32) * pair).astype(bf16)

    def collect(s, at_i, keep):
        n, m = s // steps_m, s % steps_m
        at_n = pl.ds(pl.multiple_of(n * tn, tn), tn)
        at_m = pl.ds(pl.multiple_of(m * tm, tm), tm)
        back = jnp.dot(occ[at_i, at_m], tiles[s % 2], preferred_element_type=f32)
        summed = jnp.where(m == 0, 0.0, acc[at_i, at_n]) + back
        if keep:
            acc[at_i, at_n] = summed
        rear[at_i, at_n] = summed.astype(bf16)

    @pl.loop(0, last)
    def _(s):
        tile_copy(s).wait()
        tile_copy(s + 1).start()
        screen(s)
        collect(s, pl.ds(0, no), True)

    tile_copy(last).wait()
    screen(last)
    bands = 2 if nr % 2 == 0 else 1
    tall = no // bands

    def band(ref, d, h):
        return ref.at[d, pl.ds(h * tall, tall)]

    def to_partner(d, h):
        return remote(band(core_out, d, h), band(core_in, d, h), sa.at[d, h], ra.at[d, h], pc=partner)

    def to_chip(d, h):
        return remote(
            band(plane_out, d, h), band(plane_in, d, h), sb.at[d, h], rb.at[d, h],
            pc=chip_at(d) * CORES + core,
        )

    def along(d):
        return remote(line_out.at[d], line_in.at[d], sc.at[d], rc.at[d], pr=(r + d) % nr)

    def fold(h, d):
        at = pl.ds(h * tall, tall)
        to_partner(d, h).wait_recv()
        summed = parts[d, core, at] + core_in[d, at].astype(f32)
        if d:
            plane_out[d, at] = summed.astype(bf16)
            start(to_chip(d, h))
        else:
            kept[at] = summed

    def product(h, d):
        q = chip_at(d)
        return lax.dot_general(
            rear[h * tall : (h + 1) * tall], virt[pl.ds(pl.multiple_of(q * wide, wide), wide), :],
            (((1,), (1,)), ((), ())), preferred_element_type=f32,
        )

    ranks = [*order, 0]
    pieces = [(h, ranks[g : g + 2]) for h in range(bands) for g in range(0, chips, 2)]

    def fold_piece(h, group):
        for d in group:
            fold(h, d)

    for p, (h, group) in enumerate(pieces):
        at = pl.ds(h * tall, tall)
        if group[0] == ranks[0]:
            collect(last, at, False)
        terms = [product(h, d) for d in group]
        for d, term in zip(group, terms):
            for k in range(CORES):
                parts[d, k, at] = term[:, k * cols : (k + 1) * cols]
            core_out[d, at] = parts[d, 1 - core, at].astype(bf16)
        for d in group:
            start(to_partner(d, h))
        if p >= 1:
            fold_piece(*pieces[p - 1])
    for piece in pieces[-1:]:
        fold_piece(*piece)
    for h in range(bands):
        at = pl.ds(h * tall, tall)
        for d in order:
            to_chip(d, h).wait_recv()
            kept[at] += plane_in[d, at].astype(f32)
        for d in range(1, nr):
            i = (r + d) % nr

            @pl.when(i // (nr // bands) == h)
            def _():
                line_out[d] = kept[pl.ds(pl.multiple_of(i * rows, rows), rows)].astype(bf16)
                along(d).start()

    total = kept[pl.ds(pl.multiple_of(r * rows, rows), rows)]
    for d in range(1, nr):
        along(d).wait_recv()
        total = total + line_in[d].astype(f32)
    out_ref[...] = total
    for d in range(1, nr):
        along(d).wait_send()
    for copy in sends:
        copy.wait_send()


def fused(nr, nc, iterate, occ, virt, screening):
    rows, cols = iterate.shape
    no, nv, chips = nr * rows, nc * cols, nc // CORES
    tall, long = screening.shape
    tm, tn = min(2048, tall), min(1024, long)
    dma, bf16, f32 = pltpu.SemaphoreType.DMA, jnp.bfloat16, jnp.float32
    vmem = pltpu.VMEM
    return pl.pallas_call(
        functools.partial(fused_kernel, nr, nc, tm, tn),
        out_shape=jax.ShapeDtypeStruct((rows, cols), f32),
        in_specs=[pl.BlockSpec(memory_space=pltpu.VMEM)] + [pl.BlockSpec(memory_space=pl.ANY)] * 3,
        out_specs=pl.BlockSpec(memory_space=pltpu.VMEM),
        scratch_shapes=[
            vmem((no, tall), bf16),
            vmem((tall, no), bf16),
            vmem((nv, long), bf16),
            *[vmem((no, long), bf16)] * 2,
            vmem((no, long), f32),
            vmem((2, tm, tn), bf16),
            vmem((chips, no, CORES * cols), bf16),
            vmem((chips, CORES, no, cols), f32),
            *[vmem((chips, no, cols), bf16)] * 4,
            *[vmem((nr, rows, cols), bf16)] * 2,
            vmem((no, cols), f32),
            dma((2,)),
            dma((2,)),
            dma,
            *[dma((nr,))] * 2,
            *[dma((chips, nr))] * 4,
            *[dma((chips, 2))] * 4,
            *[dma((nr,))] * 2,
        ],
        compiler_params=pltpu.CompilerParams(
            collective_id=0, has_side_effects=True, vmem_limit_bytes=63 << 20
        ),
        name="fused",
    )(iterate, occ, virt, screening)


def fits(nr, nc, iterate, screening):
    rows, cols = iterate.shape
    chips = nc // CORES
    return nc % CORES == 0 and chips > 1 and chips & (chips - 1) == 0 and rows % 16 == 0 and cols % 128 == 0


def solution(mesh):
    nr, nc = mesh.shape["pr"], mesh.shape["pc"]

    def on_device(iterate, previous, right_side, energy_gap, occ_points, virt_points, screening):
        if fits(nr, nc, iterate, screening):
            kernel = fused(nr, nc, iterate, occ_points, virt_points, screening)
            current = iterate.astype(jnp.float32)
            residual = right_side - energy_gap * current - kernel
            return (
                current
                + relax_weight * residual / energy_gap
                + momentum * (current - previous.astype(jnp.float32))
            )
        full = gather(nr, nc, iterate)
        terms = field(nc, full, occ_points, virt_points, screening)
        return reduce_update(nr, nc, terms, iterate, previous, right_side, energy_gap)

    return jax.shard_map(
        on_device,
        mesh=mesh,
        in_specs=(
            P("pr", "pc"),
            P("pr", "pc"),
            P("pr", "pc"),
            P("pr", "pc"),
            P(None, "pr"),
            P(None, "pc"),
            P("pr", "pc"),
        ),
        out_specs=P("pr", "pc"),
        check_vma=False,
    )
```
